512 devices in a mesh: ctx: 16 (over z_hi, y), dp: 32 (over z_lo, x, core).
Axes of the slice: x: 4, y: 8, z: 8 (z_hi: 2, z_lo: 4; z = z_hi * 4 + z_lo), core: 2. Of those that a mesh axis runs over, the one named last changes fastest.
Arguments:
- queries: bfloat16 [32, 2048, 2048], P('dp', 'ctx'), may hold values from -8 to 8
- key_rows: bfloat16 [32, 2048, 256], P('dp', 'ctx'), may hold values from -8 to 8
- value_rows: bfloat16 [32, 2048, 256], P('dp', 'ctx'), may hold values from -6 to 6
- stream: bfloat16 [32, 2048, 2048], P('dp', 'ctx'), may hold values from -6 to 6
- norm_gain: float32 [2048], replicated, may hold values from 0.1 to 1.9
- expert_ids: int32 [32, 2048, 8], P('dp', 'ctx'), may hold values from 0 to 127, all different within a row; in each aligned block of 128 rows (0 to 127, 128 to 255, ..., all dimensions but the last counted through in order) at most 12 rows name the same one
- gate_values: float32 [32, 2048, 8], P('dp', 'ctx'), may hold values from 0.1 to 1
- w_gate: bfloat16 [32, 2048, 384], P('dp', 'ctx'), may hold values from -0.125 to 0.125
- w_up: bfloat16 [32, 2048, 384], P('dp', 'ctx'), may hold values from -0.125 to 0.125
- w_down: bfloat16 [32, 384, 2048], P('dp', None, 'ctx'), may hold values from -0.3125 to 0.3125
Outputs:
- attended: bfloat16 [32, 2048, 2048], P('dp', 'ctx')
- expert_out: bfloat16 [32, 2048, 2048], P('dp', 'ctx')
The draws below stay inside these ranges and needn't reach their ends.
Inputs may be any that keep to these rules, and one draw needn't show every extreme that they name: `expert_ids`: among the rows of one device, no expert is chosen by more than 12 rows; some expert reaches 12.
All inputs are finite; a program needn't handle non-finite values.
Results may differ from the reference program's by a relative error of at most 0.012.
Values may be sent and summed in bfloat16 or wider, within the bound.
No kernel may reach another device: no remote copies, remote signals or barrier semaphores. Data moves between devices by JAX's collectives and lax.ppermute only.
A program may use at most 64 MiB of HBM per device.

```python
import math
import jax
import jax.numpy as jnp
import numpy as np
from jax import lax

D = 2048
HD = 128
EXPERTS = 128
TOP = 8
QH = 16
KVH = 2
EXP_HID = 384
TOK_DEV = 128
LENGTH = 2048
SEQS = 32
FLIGHT = 32
CAP = 12
N_CTX = 16


def paired_fields(key):
    query_key = jax.random.fold_in(key, 11)
    other_key = jax.random.fold_in(key, 23)
    queries = jnp.clip(jax.random.normal(query_key, (SEQS, LENGTH, QH * HD), jnp.float32), -4.0, 4.0)
    keyset = jnp.clip(jax.random.normal(other_key, (SEQS, LENGTH, KVH * HD), jnp.float32), -4.0, 4.0)
    return (queries, keyset)


def draw_queries(key, part):
    return paired_fields(key)[0].astype(jnp.bfloat16)


def draw_key_rows(key, part):
    return paired_fields(key)[1].astype(jnp.bfloat16)


def block_scale(key, extent, shards, least, high):
    def one(dim, blocks):
        draws = jax.random.uniform(jax.random.fold_in(jax.random.fold_in(key, 6), dim), (blocks,), jnp.float32, least / len(shards), high / len(shards))
        return jnp.repeat(jnp.exp(draws), extent[dim] // blocks).reshape((-1,) + (1,) * (len(extent) - dim - 1))

    loudness = one(*shards[0])
    for cut in shards[1:]:
        loudness = loudness * one(*cut)
    return loudness


def routed_block(rng, own, number, rows, amount, top, most, lean):
    sequence = jax.random.permutation(rng, amount)
    heavy_load, usual = load_shares(amount, rows * top, most, lean, True), load_shares(amount, rows * top, most, lean, False)
    places = jnp.arange(amount)

    def named(lengths, offset_by):
        used = int((lengths > 0).sum())
        fixed = max(1, used // 4)
        passed = fixed + (places - fixed + offset_by * (used - fixed)) % max(1, amount - fixed)
        return jnp.zeros((amount,), jnp.int32).at[sequence[jnp.where(places < fixed, places, passed)]].set(jnp.asarray(lengths, jnp.int32))

    lengths = jnp.where(number % 4 == 0, named(heavy_load, number // 4), named(usual, number - number // 4 - 1))
    mixed = jax.random.permutation(jax.random.fold_in(own, 3), amount)
    giver, receiver = mixed[0:amount // 2 * 2:2], mixed[1:amount // 2 * 2:2]
    margin = jnp.minimum(lengths[giver] - 1, most - lengths[receiver]) // 2
    margin = jnp.where((giver == sequence[0]) | (receiver == sequence[0]) | (lengths[receiver] == 0), 0, jnp.maximum(margin, 0))
    passed = jax.random.randint(jax.random.fold_in(own, 4), (amount // 2,), 0, 1 << 20) % (margin + 1)
    lengths = lengths.at[giver].add(-passed).at[receiver].add(passed)
    members = jnp.searchsorted(jnp.cumsum(lengths), jnp.arange(rows * top), side="right").astype(jnp.int32)
    table = members.reshape(top, rows).T
    table = table[jax.random.permutation(jax.random.fold_in(own, 1), rows)]
    offset_by = jax.random.randint(jax.random.fold_in(own, 2), (rows, 1), 0, top)
    return jnp.take_along_axis(table, (jnp.arange(top)[None, :] + offset_by) % top, axis=1)


def load_shares(number_of, total, most, skew, full):
    loads = [(1 << 20) // math.isqrt(grade ** skew) + 1 for grade in range(1, number_of + 1)]
    largest = most if full else min(most, max(-(-total // number_of), total * loads[0] // sum(loads)))
    least = 1 if total - largest >= number_of - 1 else 0
    given, spare = [largest] + [least] * (number_of - 1), total - largest - least * (number_of - 1)
    while spare > 0:
        free = [i for i in range(1, number_of) if given[i] < largest] or [i for i in range(1, number_of) if given[i] < most]
        mass, budget = sum([loads[i] for i in free]), spare
        for i in free:
            addition = min(most - given[i], max(1, budget * loads[i] // mass), spare)
            given[i] = given[i] + addition
            spare = spare - addition
    return np.array(given)


def bell_draw(stream_key, dims, deviation, reach, split=(), held_as=jnp.bfloat16):
    array = deviation * jax.random.normal(stream_key, dims, jnp.float32)
    if split:
        array = array * block_scale(stream_key, dims, split, -0.22, 0.18)
    return jnp.clip(array, -reach, reach).astype(held_as)


def setup_inputs(seed: int = 0) -> dict:
    splits = jax.random.split(jax.random.key(seed), 11)
    queries = draw_queries(jax.random.fold_in(splits[10], 71), 0)
    key_rows = draw_key_rows(jax.random.fold_in(splits[10], 71), 0)
    value_rows = bell_draw(splits[2], (SEQS, LENGTH, KVH * HD), 1.0, 6.0, ((0, 32), (1, 16)))
    stream = bell_draw(splits[3], (SEQS, LENGTH, D), 1.0, 6.0, ((0, 32), (1, 16)))
    norm_gain = jnp.clip(1.0 + 0.18 * jax.random.normal(splits[4], (D,), jnp.float32), 0.1, 1.9)
    expert_ids_keys = jax.random.split(jax.random.fold_in(splits[5], 1), SEQS * LENGTH // TOK_DEV)
    expert_ids_turns = jax.random.permutation(jax.random.fold_in(splits[5], 3), SEQS * LENGTH // TOK_DEV)
    expert_ids = jax.vmap(lambda own, number: routed_block(jax.random.fold_in(splits[5], 2), own, number, TOK_DEV, EXPERTS, TOP, CAP, 1))(expert_ids_keys, expert_ids_turns).reshape((SEQS, LENGTH, TOP))
    gate_values = jnp.clip(jnp.exp(math.log(1.0) - 2.3025851 * jax.random.uniform(splits[6], (SEQS, LENGTH, TOP), jnp.float32) ** block_scale(splits[6], (SEQS, LENGTH, TOP), ((0, 32), (1, 16)), -0.2, 0.2)), 0.1, 1.0)
    w_gate = bell_draw(splits[7], (FLIGHT, D, EXP_HID), D ** -0.5, 0.125, ((0, 32), (1, 16)))
    w_up = bell_draw(splits[8], (FLIGHT, D, EXP_HID), D ** -0.5, 0.125, ((0, 32), (1, 16)))
    w_down = bell_draw(splits[9], (FLIGHT, EXP_HID, D), EXP_HID ** -0.5, 0.3125, ((0, 32), (2, 16)))
    return {"queries": queries, "key_rows": key_rows, "value_rows": value_rows, "stream": stream, "norm_gain": norm_gain, "expert_ids": expert_ids, "gate_values": gate_values, "w_gate": w_gate, "w_up": w_up, "w_down": w_down}


def attend_sequence(operands):
    query_seq, key_seq, value_seq = operands
    group = QH // KVH
    scale = 1.0 / math.sqrt(HD)
    positions = jnp.arange(LENGTH, dtype=jnp.int32)
    allowed = positions[None, :] <= positions[:, None]
    query_heads = query_seq.reshape(LENGTH, KVH, group, HD)
    key_heads = key_seq.reshape(LENGTH, KVH, HD)
    value_heads = value_seq.reshape(LENGTH, KVH, HD)

    def one_head(head):
        query_group = query_heads[:, head].astype(jnp.float32)
        key_group = key_heads[:, head].astype(jnp.float32)
        value_group = value_heads[:, head].astype(jnp.float32)
        scores = jnp.einsum('qgd,kd->gqk', query_group, key_group) * scale
        masked = jnp.where(allowed[None], scores, -jnp.inf)
        largest = lax.optimization_barrier(jnp.max(masked, axis=-1, keepdims=True))
        probs = jnp.where(allowed[None], jnp.exp(scores - largest), 0.0)
        total = lax.optimization_barrier(jnp.sum(probs, axis=-1))
        rounded = probs.astype(jnp.bfloat16).astype(jnp.float32)
        mixed = jnp.einsum('gqk,kd->gqd', rounded, value_group)
        return mixed / total[..., None]
    heads_out = lax.map(one_head, jnp.arange(KVH, dtype=jnp.int32))
    return heads_out.transpose(2, 0, 1, 3).reshape(LENGTH, QH * HD).astype(jnp.bfloat16)

def reference(queries, key_rows, value_rows, stream, norm_gain, expert_ids, gate_values, w_gate, w_up, w_down):
    attended = lax.map(attend_sequence, (queries, key_rows, value_rows))
    count = SEQS * LENGTH
    flat = stream.reshape(count, D).astype(jnp.float32)
    normed = (flat * lax.rsqrt(lax.optimization_barrier(jnp.mean(flat * flat, axis=-1, keepdims=True)) + 1e-06) * norm_gain.astype(jnp.float32)).astype(jnp.bfloat16)
    chosen_ids = expert_ids.reshape(count, TOP)
    gates = gate_values.reshape(count, TOP)
    most_rows = SEQS * N_CTX * CAP

    def expert_step(total, index):
        hits = chosen_ids == index
        weight = lax.optimization_barrier(jnp.sum(jnp.where(hits, gates, 0.0), axis=1))
        chosen = jnp.any(hits, axis=1)
        rows = jnp.nonzero(chosen, size=most_rows, fill_value=0)[0].astype(jnp.int32)
        live = jnp.arange(most_rows, dtype=jnp.int32) < jnp.sum(chosen.astype(jnp.int32))
        picked = normed[rows]
        gate = jnp.dot(picked, w_gate[index], preferred_element_type=jnp.float32)
        upper = jnp.dot(picked, w_up[index], preferred_element_type=jnp.float32)
        hidden = (jax.nn.silu(gate) * upper).astype(jnp.bfloat16)
        answer = jnp.dot(hidden, w_down[index], preferred_element_type=jnp.float32).astype(jnp.bfloat16)
        scaled = answer.astype(jnp.float32) * jnp.where(live, weight[rows], 0.0)[:, None]
        return (total.at[rows].add(scaled), None)
    start_total = jnp.zeros((count, D), jnp.float32)
    total, unused = lax.scan(expert_step, start_total, jnp.arange(FLIGHT, dtype=jnp.int32))
    expert_out = total.astype(jnp.bfloat16).reshape(SEQS, LENGTH, D)
    return (attended, expert_out)
```

```python
import functools
import math

import jax
import jax.numpy as jnp
from jax import lax
from jax.experimental import pallas as pl
from jax.experimental.pallas import tpu as pltpu
from jax.sharding import Mesh, PartitionSpec as P

HD = 128
CAP = 12
LOW = 8
FOLD = CAP - LOW
CTX = ("zh", "y")
DP = ("zl", "x", "c")
MASKED = -1e30
F32 = jnp.float32
BF16 = jnp.bfloat16
VMEM = pl.BlockSpec(memory_space=pltpu.VMEM)


def natural_block(place, halves, ring):
    return (place % halves) * ring + place // halves


def dispatch_kernel(halves, ring, owners, x_ref, gain_ref, ids_ref, gates_ref, out_ref, mix_a_ref, mix_b_ref):
    tokens, width = x_ref.shape
    slots = owners * LOW
    half = width // 2
    x = x_ref[...].astype(F32)
    normed = (x * lax.rsqrt(jnp.mean(x * x, axis=-1, keepdims=True) + 1e-06) * gain_ref[...]).astype(BF16)
    step = width // (halves * ring)
    pieces = []
    for place in range(halves * ring):
        start = natural_block(place, halves, ring) * step
        pieces.append(normed[:, start : start + step])
    normed = jnp.concatenate(pieces, axis=1)

    lane = lax.broadcasted_iota(jnp.int32, (tokens, slots), 1)
    expert = lane // LOW
    place = lane % LOW
    ids = ids_ref[...]
    gates = gates_ref[...]
    hot = jnp.zeros((tokens, slots), F32)
    gate = jnp.zeros((tokens, slots), F32)
    for k in range(ids.shape[1]):
        hit = ids[:, k : k + 1] == expert
        hot = jnp.where(hit, 1.0, hot)
        gate = jnp.where(hit, gates[:, k : k + 1], gate)
    row = lax.broadcasted_iota(jnp.int32, (tokens, tokens), 0)
    col = lax.broadcasted_iota(jnp.int32, (tokens, tokens), 1)
    earlier = jnp.where(col < row, 1.0, 0.0).astype(BF16)
    rank = jnp.dot(earlier, hot.astype(BF16), preferred_element_type=F32)
    rank = jnp.where(hot > 0.5, rank, -1.0)
    in_a = rank == place.astype(F32)
    in_b = rank == (LOW + place % FOLD).astype(F32)
    in_lo = in_b & (place < FOLD)
    in_hi = in_b & (place >= FOLD)

    def put(chosen):
        return jnp.where(chosen, 1.0, 0.0).astype(BF16)

    contract = (((0,), (0,)), ((), ()))
    out_ref[:, :width] = lax.dot_general(put(in_a), normed, contract, preferred_element_type=F32).astype(BF16)
    pick = jnp.concatenate([put(in_lo), put(in_hi)], axis=0)
    stacked = jnp.concatenate([normed[:, :half], normed[:, half:]], axis=0)
    out_ref[:, width:] = lax.dot_general(pick, stacked, contract, preferred_element_type=F32).astype(BF16)

    top = gate.astype(BF16).astype(F32)
    rest = gate - top

    def mix(chosen):
        return jnp.concatenate(
            [jnp.where(chosen, top, 0.0).astype(BF16), jnp.where(chosen, rest, 0.0).astype(BF16)], axis=0
        )

    mix_a_ref[...] = mix(in_a)
    mix_b_ref[:, :slots] = mix(in_lo)
    mix_b_ref[:, slots:] = mix(in_hi)


def expert_kernel(hidden_units, x_ref, w_ref, out_ref):
    rows, cols = x_ref.shape
    width = w_ref.shape[0] * w_ref.shape[1]
    half = width // 2
    both = 2 * hidden_units
    block = w_ref.shape[1]
    count = w_ref.shape[0]

    def part(lo, hi):
        return w_ref[lo:hi, :, :both].reshape((hi - lo) * block, both)

    low_w = part(0, count // 2)
    high_w = part(count // 2, count)
    sums_a = jnp.dot(x_ref[:, :half], low_w, preferred_element_type=F32)
    sums_a = sums_a + jnp.dot(x_ref[:, half:width], high_w, preferred_element_type=F32)
    folded = x_ref[:, width:]
    first = lax.broadcasted_iota(jnp.int32, (rows, both), 0) % LOW < FOLD
    sums_b = jnp.where(
        first,
        jnp.dot(folded, low_w, preferred_element_type=F32),
        jnp.dot(folded, high_w, preferred_element_type=F32),
    )
    groups = sums_b.reshape(rows // LOW, LOW, both)
    sums_b = (groups + pltpu.roll(groups, FOLD, 1)).reshape(rows, both)

    def activate(sums):
        gate = sums[:, :hidden_units]
        return (gate / (1.0 + jnp.exp(-gate)) * sums[:, hidden_units:]).astype(BF16)

    hidden_a = activate(sums_a)
    hidden_b = activate(sums_b)

    def down(place):
        pieces = [w_ref[place, :, both + j * block : both + (j + 1) * block] for j in range(hidden_units // block)]
        return jnp.concatenate(pieces, axis=0)

    first_out = lax.broadcasted_iota(jnp.int32, (rows, 2 * block), 0) % LOW < FOLD
    for pair in range(count // 4):
        lo, hi = 2 * pair, count // 2 + 2 * pair
        low_d = jnp.concatenate([down(lo), down(lo + 1)], axis=1)
        high_d = jnp.concatenate([down(hi), down(hi + 1)], axis=1)
        out_ref[:, lo * block : (lo + 2) * block] = jnp.dot(
            hidden_a, low_d, preferred_element_type=F32
        ).astype(BF16)
        out_ref[:, hi * block : (hi + 2) * block] = jnp.dot(
            hidden_a, high_d, preferred_element_type=F32
        ).astype(BF16)
        out_ref[:, width + lo * block : width + (lo + 2) * block] = jnp.where(
            first_out,
            jnp.dot(hidden_b, low_d, preferred_element_type=F32),
            jnp.dot(hidden_b, high_d, preferred_element_type=F32),
        ).astype(BF16)


def combine_kernel(halves, ring, back_ref, mix_a_ref, mix_b_ref, out_ref):
    tokens, width = out_ref.shape
    half = width // 2
    slots = back_ref.shape[0]
    step = width // (halves * ring)
    folded = back_ref[:, width:]
    for side in range(2):
        both = jnp.dot(
            mix_a_ref[...], back_ref[:, side * half : (side + 1) * half], preferred_element_type=F32
        ) + jnp.dot(
            mix_b_ref[:, side * slots : (side + 1) * slots], folded, preferred_element_type=F32
        )
        total = (both[:tokens] + both[tokens:]).astype(BF16)
        for i in range(half // step):
            start = natural_block(side * (half // step) + i, halves, ring) * step
            out_ref[:, start : start + step] = total[:, i * step : (i + 1) * step]


def attend_kernel(halves, ring, heads_kv, q_ref, kv_ref, place_ref, out_ref):
    tokens, wide = q_ref.shape
    heads = wide // HD
    group = heads // heads_kv
    blocks = kv_ref.shape[0]
    keys = blocks * kv_ref.shape[1]
    scale = 1.0 / math.sqrt(HD)
    lane = lax.broadcasted_iota(jnp.int32, (tokens, keys), 1)
    row = lax.broadcasted_iota(jnp.int32, (tokens, keys), 0)
    block = lane // tokens
    key_pos = ((block % halves) * ring + block // halves) * tokens + lane % tokens
    allowed = key_pos <= row + place_ref[0] * tokens
    for g in range(heads_kv):
        key = kv_ref[:, :, g * HD : (g + 1) * HD].reshape(keys, HD)
        value = kv_ref[:, :, (heads_kv + g) * HD : (heads_kv + g + 1) * HD].reshape(keys, HD)

        @pl.loop(0, group)
        def _(i):
            at = pl.ds(pl.multiple_of((g * group + i) * HD, HD), HD)
            scores = lax.dot_general(
                q_ref[:, at], key, (((1,), (1,)), ((), ())), preferred_element_type=F32
            )
            scores = jnp.where(allowed, scores * scale, MASKED)
            largest = jnp.max(scores, axis=-1, keepdims=True)
            probs = jnp.exp(scores - largest)
            total = jnp.sum(probs, axis=-1, keepdims=True)
            mixed = jnp.dot(probs.astype(BF16), value, preferred_element_type=F32)
            out_ref[:, at] = (mixed / total).astype(BF16)


def estimate(flops, bytes_accessed, transcendentals=0):
    return pl.CostEstimate(flops=flops, bytes_accessed=bytes_accessed, transcendentals=transcendentals)


def shards(
    queries, key_rows, value_rows, stream, norm_gain, expert_ids, gate_values, w_gate, w_up, w_down
):
    tokens, width = stream.shape[1:]
    heads_kv = key_rows.shape[2] // HD
    hidden_units = w_gate.shape[2]
    halves, ring = lax.axis_size("zh"), lax.axis_size("y")
    owners = lax.axis_size(DP)
    slots = owners * LOW
    wide = width + width // 2
    params = pltpu.CompilerParams(vmem_limit_bytes=48 * 1024 * 1024)

    with jax.named_scope("weights"):
        down = w_down[0]
        pieces = [down[j * tokens : (j + 1) * tokens] for j in range(hidden_units // tokens)]
        packed = jnp.concatenate([w_gate[0], w_up[0]] + pieces, axis=1)
        pair = lax.all_gather(packed, "zh", axis=0)
        weights = lax.all_gather(pair, "y", axis=0, tiled=True)

    with jax.named_scope("dispatch"):
        ids, pair = lax.optimization_barrier((expert_ids[0], pair))
        outgoing, mix_a, mix_b = pl.pallas_call(
            functools.partial(dispatch_kernel, halves, ring, owners),
            out_shape=(
                jax.ShapeDtypeStruct((slots, wide), BF16),
                jax.ShapeDtypeStruct((2 * tokens, slots), BF16),
                jax.ShapeDtypeStruct((2 * tokens, 2 * slots), BF16),
            ),
            in_specs=[VMEM] * 4,
            out_specs=(VMEM,) * 3,
            compiler_params=params,
            cost_estimate=estimate(4 * 256 * 256 * 2048, 4 * 1024 * 1024),
            name="dispatch",
        )(stream[0], norm_gain[None, :], ids, gate_values[0])
        arrived = lax.all_to_all(
            outgoing.reshape(owners, LOW, wide), DP, split_axis=0, concat_axis=0, tiled=True
        ).reshape(slots, wide)

    with jax.named_scope("keys"):
        kv = jnp.concatenate([key_rows[0], value_rows[0]], axis=1)
        kv, outgoing = lax.optimization_barrier((kv, outgoing))
        kv_pair = lax.all_gather(kv, "zh", axis=0)
        kv_all = lax.all_gather(kv_pair, "y", axis=0, tiled=True)

    with jax.named_scope("experts"):
        answers = pl.pallas_call(
            functools.partial(expert_kernel, hidden_units),
            out_shape=jax.ShapeDtypeStruct((slots, wide), BF16),
            in_specs=[VMEM] * 2,
            out_specs=VMEM,
            compiler_params=params,
            cost_estimate=estimate(6 * 512 * 2048 * 384, 8 * 1024 * 1024),
            name="experts",
        )(arrived, weights)
        returned = lax.all_to_all(
            answers.reshape(owners, LOW, wide), DP, split_axis=0, concat_axis=0, tiled=True
        ).reshape(slots, wide)

    with jax.named_scope("attend"):
        place = lax.axis_index(CTX).astype(jnp.int32)[None]
        attended = pl.pallas_call(
            functools.partial(attend_kernel, halves, ring, heads_kv),
            out_shape=jax.ShapeDtypeStruct(queries.shape[1:], BF16),
            in_specs=[VMEM, VMEM, pl.BlockSpec(memory_space=pltpu.SMEM)],
            out_specs=VMEM,
            compiler_params=params,
            cost_estimate=estimate(4 * 2048 * 128 * 2048, 4 * 1024 * 1024, 16 * 128 * 2048),
            name="attend",
        )(queries[0], kv_all, place)

    with jax.named_scope("combine"):
        expert_out = pl.pallas_call(
            functools.partial(combine_kernel, halves, ring),
            out_shape=jax.ShapeDtypeStruct((tokens, width), BF16),
            in_specs=[VMEM] * 3,
            out_specs=VMEM,
            compiler_params=params,
            cost_estimate=estimate(2 * 256 * 512 * 2048, 3 * 1024 * 1024),
            name="combine",
        )(returned, mix_a, mix_b)
    return (attended[None], expert_out[None])


def solution(mesh):
    fine = Mesh(mesh.devices.reshape(2, 8, 4, 4, 2), CTX + DP)
    rows = P(DP, CTX, None)
    return jax.shard_map(
        shards,
        mesh=fine,
        in_specs=(rows, rows, rows, rows, P(), rows, rows, rows, rows, P(DP, None, CTX)),
        out_specs=(rows, rows),
        check_vma=False,
    )
```

```python
import functools
import math

import jax
import jax.numpy as jnp
from jax import lax
from jax.experimental import pallas as pl
from jax.experimental.pallas import tpu as pltpu
from jax.sharding import Mesh, PartitionSpec as P

HD = 128
CAP = 12
LOW = 8
FOLD = CAP - LOW
CTX = ("zh", "y")
DP = ("zl", "x", "c")
CHIPS = ("zh", "zl", "x")
MASKED = -1e30
F32 = jnp.float32
BF16 = jnp.bfloat16
VMEM = pl.BlockSpec(memory_space=pltpu.VMEM)
SMEM = pl.BlockSpec(memory_space=pltpu.SMEM)


def pack_kernel(gate_ref, up_ref, down_ref, out_ref):
    rows, units = gate_ref.shape
    out_ref[:, :units] = gate_ref[...]
    out_ref[:, units : 2 * units] = up_ref[...]
    for j in range(units // rows):
        out_ref[:, (2 * units + j * rows) : (2 * units + (j + 1) * rows)] = down_ref[j * rows : (j + 1) * rows, :]


def dispatch_kernel(halves, owners, x_ref, gain_ref, ids_ref, gates_ref, out_ref, mix_a_ref, mix_b_ref):
    tokens, width = x_ref.shape
    slots = owners * LOW
    half = width // 2
    x = x_ref[...].astype(F32)
    normed = (x * lax.rsqrt(jnp.mean(x * x, axis=-1, keepdims=True) + 1e-06) * gain_ref[...]).astype(BF16)
    lane = lax.broadcasted_iota(jnp.int32, (tokens, slots), 1)
    chip = lane // LOW
    per_half = owners // halves
    expert = chip % per_half * halves + chip // per_half
    place = lane % LOW
    ids = ids_ref[...]
    gates = gates_ref[...]
    hot = jnp.zeros((tokens, slots), F32)
    gate = jnp.zeros((tokens, slots), F32)
    for k in range(ids.shape[1]):
        hit = ids[:, k : k + 1] == expert
        hot = jnp.where(hit, 1.0, hot)
        gate = jnp.where(hit, gates[:, k : k + 1], gate)
    row = lax.broadcasted_iota(jnp.int32, (tokens, tokens), 0)
    col = lax.broadcasted_iota(jnp.int32, (tokens, tokens), 1)
    earlier = jnp.where(col < row, 1.0, 0.0).astype(BF16)
    rank = jnp.dot(earlier, hot.astype(BF16), preferred_element_type=F32)
    rank = jnp.where(hot > 0.5, rank, -1.0)
    in_a = rank == place.astype(F32)
    in_b = rank == (LOW + place % FOLD).astype(F32)
    in_lo = in_b & (place < FOLD)
    in_hi = in_b & (place >= FOLD)

    def put(chosen):
        return jnp.where(chosen, 1.0, 0.0).astype(BF16)

    contract = (((0,), (0,)), ((), ()))
    out_ref[:, :width] = lax.dot_general(put(in_a), normed, contract, preferred_element_type=F32).astype(BF16)
    pick = jnp.concatenate([put(in_lo), put(in_hi)], axis=0)
    stacked = jnp.concatenate([normed[:, :half], normed[:, half:]], axis=0)
    out_ref[:, width:] = lax.dot_general(pick, stacked, contract, preferred_element_type=F32).astype(BF16)

    top = gate.astype(BF16).astype(F32)
    rest = gate - top

    def mix(chosen):
        return jnp.concatenate(
            [jnp.where(chosen, top, 0.0).astype(BF16), jnp.where(chosen, rest, 0.0).astype(BF16)], axis=0
        )

    mix_a_ref[...] = mix(in_a)
    mix_b_ref[:, :slots] = mix(in_lo)
    mix_b_ref[:, slots:] = mix(in_hi)


def expert_kernel(hidden_units, x_ref, mine_ref, other_ref, core_ref, out_ref):
    rows, wide = x_ref.shape
    count, block = mine_ref.shape[:2]
    half = count * block
    width = 2 * half
    both = 2 * hidden_units
    core = core_ref[0]
    mine_at = pl.multiple_of(core * half, half)
    other_at = pl.multiple_of((1 - core) * half, half)

    mine_w = mine_ref[:, :, :both].reshape(half, both)
    other_w = other_ref[:, :, :both].reshape(half, both)
    sums_a = jnp.dot(x_ref[:, pl.ds(mine_at, half)], mine_w, preferred_element_type=F32)
    sums_a = sums_a + jnp.dot(x_ref[:, pl.ds(other_at, half)], other_w, preferred_element_type=F32)
    folded = x_ref[:, width:]

    def from_mine(columns):
        side = lax.broadcasted_iota(jnp.int32, (rows, columns), 0) % LOW // FOLD
        return side == core

    sums_b = jnp.where(
        from_mine(both),
        jnp.dot(folded, mine_w, preferred_element_type=F32),
        jnp.dot(folded, other_w, preferred_element_type=F32),
    )
    groups = sums_b.reshape(rows // LOW, LOW, both)
    sums_b = (groups + pltpu.roll(groups, FOLD, 1)).reshape(rows, both)

    def activate(sums):
        gate = sums[:, :hidden_units]
        return (gate / (1.0 + jnp.exp(-gate)) * sums[:, hidden_units:]).astype(BF16)

    hidden_a = activate(sums_a)
    hidden_b = activate(sums_b)

    def down(ref, place):
        pieces = [ref[place, :, both + j * block : both + (j + 1) * block] for j in range(hidden_units // block)]
        return jnp.concatenate(pieces, axis=0)

    for lo in range(0, count, 2):
        mine_d = jnp.concatenate([down(mine_ref, lo), down(mine_ref, lo + 1)], axis=1)
        other_d = jnp.concatenate([down(other_ref, lo), down(other_ref, lo + 1)], axis=1)
        at, columns = lo * block, 2 * block
        out_ref[:, pl.ds(pl.multiple_of(mine_at + at, columns), columns)] = jnp.dot(
            hidden_a, mine_d, preferred_element_type=F32
        ).astype(BF16)
        out_ref[:, pl.ds(pl.multiple_of(other_at + at, columns), columns)] = jnp.dot(
            hidden_a, other_d, preferred_element_type=F32
        ).astype(BF16)
        out_ref[:, width + at : width + at + columns] = jnp.where(
            from_mine(columns),
            jnp.dot(hidden_b, mine_d, preferred_element_type=F32),
            jnp.dot(hidden_b, other_d, preferred_element_type=F32),
        ).astype(BF16)


def combine_kernel(back_ref, mix_a_ref, mix_b_ref, out_ref):
    tokens, width = out_ref.shape
    half = width // 2
    slots = back_ref.shape[0]
    folded = back_ref[:, width:]
    for side in range(2):
        columns = slice(side * half, (side + 1) * half)
        both = jnp.dot(mix_a_ref[...], back_ref[:, columns], preferred_element_type=F32) + jnp.dot(
            mix_b_ref[:, side * slots : (side + 1) * slots], folded, preferred_element_type=F32
        )
        out_ref[:, columns] = (both[:tokens] + both[tokens:]).astype(BF16)


def attend_kernel(halves, ring, heads_kv, q_ref, kv_ref, place_ref, out_ref):
    tokens, wide = q_ref.shape
    heads = wide // HD
    group = heads // heads_kv
    blocks = kv_ref.shape[0]
    keys = blocks * kv_ref.shape[1]
    scale = 1.0 / math.sqrt(HD)
    lane = lax.broadcasted_iota(jnp.int32, (tokens, keys), 1)
    row = lax.broadcasted_iota(jnp.int32, (tokens, keys), 0)
    block = lane // tokens
    here = place_ref[0] // ring
    passed = jnp.where(here == 0, halves, 0)
    side = jnp.where(block % halves == 0, here, passed)
    key_pos = (side * ring + block // halves) * tokens + lane % tokens
    allowed = key_pos <= row + place_ref[0] * tokens
    for g in range(heads_kv):
        key = kv_ref[:, :, g * HD : (g + 1) * HD].reshape(keys, HD)
        value = kv_ref[:, :, (heads_kv + g) * HD : (heads_kv + g + 1) * HD].reshape(keys, HD)

        @pl.loop(0, group)
        def _(i):
            at = pl.ds(pl.multiple_of((g * group + i) * HD, HD), HD)
            scores = lax.dot_general(
                q_ref[:, at], key, (((1,), (1,)), ((), ())), preferred_element_type=F32
            )
            scores = jnp.where(allowed, scores * scale, MASKED)
            largest = jnp.max(scores, axis=-1, keepdims=True)
            probs = jnp.exp(scores - largest)
            total = jnp.sum(probs, axis=-1, keepdims=True)
            mixed = jnp.dot(probs.astype(BF16), value, preferred_element_type=F32)
            out_ref[:, at] = (mixed / total).astype(BF16)


def estimate(flops, bytes_accessed, transcendentals=0):
    return pl.CostEstimate(flops=flops, bytes_accessed=bytes_accessed, transcendentals=transcendentals)


def shards(
    queries, key_rows, value_rows, stream, norm_gain, expert_ids, gate_values, w_gate, w_up, w_down
):
    tokens, width = stream.shape[1:]
    heads_kv = key_rows.shape[2] // HD
    hidden_units = w_gate.shape[2]
    halves, ring, cores = lax.axis_size("zh"), lax.axis_size("y"), lax.axis_size("c")
    owners = lax.axis_size(DP)
    slots = owners * LOW
    wide = width + width // 2
    params = pltpu.CompilerParams(vmem_limit_bytes=48 * 1024 * 1024)

    with jax.named_scope("weights"):
        packed = pl.pallas_call(
            pack_kernel,
            out_shape=jax.ShapeDtypeStruct((w_gate.shape[1], 3 * hidden_units), BF16),
            in_specs=[VMEM] * 3,
            out_specs=VMEM,
            name="pack",
        )(w_gate[0], w_up[0], w_down[0])
        swap = [(h * cores + c, c * cores + h) for h in range(halves) for c in range(cores)]
        kv = jnp.concatenate([key_rows[0], value_rows[0]], axis=1)
        kv, packed = lax.optimization_barrier((kv, packed))
        mine_part = lax.ppermute(packed, ("zh", "c"), swap)
        kv_passed = lax.ppermute(kv, "zh", [(0, 1)])
        mine = lax.all_gather(mine_part, "y", axis=0)
        other = lax.ppermute(mine, "c", [(0, 1), (1, 0)])

    with jax.named_scope("dispatch"):
        ids, _, kv_passed = lax.optimization_barrier((expert_ids[0], mine_part, kv_passed))
        outgoing, mix_a, mix_b = pl.pallas_call(
            functools.partial(dispatch_kernel, halves, owners),
            out_shape=(
                jax.ShapeDtypeStruct((slots, wide), BF16),
                jax.ShapeDtypeStruct((2 * tokens, slots), BF16),
                jax.ShapeDtypeStruct((2 * tokens, 2 * slots), BF16),
            ),
            in_specs=[VMEM] * 4,
            out_specs=(VMEM,) * 3,
            compiler_params=params,
            cost_estimate=estimate(4 * 256 * 256 * 2048, 4 * 1024 * 1024),
            name="dispatch",
        )(stream[0], norm_gain[None, :], ids, gate_values[0])
        arrived = lax.all_to_all(
            outgoing.reshape(owners, LOW, wide), CHIPS, split_axis=0, concat_axis=0, tiled=True
        ).reshape(slots, wide)

    with jax.named_scope("keys"):
        kv_passed, outgoing = lax.optimization_barrier((kv_passed, outgoing))
        kv_pair = jnp.stack([kv, kv_passed])
        kv_all = lax.all_gather(kv_pair, "y", axis=0, tiled=True)

    with jax.named_scope("experts"):
        answers = pl.pallas_call(
            functools.partial(expert_kernel, hidden_units),
            out_shape=jax.ShapeDtypeStruct((slots, wide), BF16),
            in_specs=[VMEM, VMEM, VMEM, SMEM],
            out_specs=VMEM,
            compiler_params=params,
            cost_estimate=estimate(6 * 512 * 2048 * 384, 8 * 1024 * 1024),
            name="experts",
        )(arrived, mine, other, lax.axis_index("c").astype(jnp.int32)[None])
        returned = lax.all_to_all(
            answers.reshape(owners, LOW, wide), CHIPS, split_axis=0, concat_axis=0, tiled=True
        ).reshape(slots, wide)

    with jax.named_scope("attend"):
        place = lax.axis_index(CTX).astype(jnp.int32)[None]
        attended = pl.pallas_call(
            functools.partial(attend_kernel, halves, ring, heads_kv),
            out_shape=jax.ShapeDtypeStruct(queries.shape[1:], BF16),
            in_specs=[VMEM, VMEM, SMEM],
            out_specs=VMEM,
            compiler_params=params,
            cost_estimate=estimate(4 * 2048 * 128 * 2048, 4 * 1024 * 1024, 16 * 128 * 2048),
            name="attend",
        )(queries[0], kv_all, place)

    with jax.named_scope("combine"):
        expert_out = pl.pallas_call(
            combine_kernel,
            out_shape=jax.ShapeDtypeStruct((tokens, width), BF16),
            in_specs=[VMEM] * 3,
            out_specs=VMEM,
            compiler_params=params,
            cost_estimate=estimate(2 * 256 * 512 * 2048, 3 * 1024 * 1024),
            name="combine",
        )(returned, mix_a, mix_b)
    return (attended[None], expert_out[None])


def solution(mesh):
    fine = Mesh(mesh.devices.reshape(2, 8, 4, 4, 2), CTX + DP)
    rows = P(DP, CTX, None)
    return jax.shard_map(
        shards,
        mesh=fine,
        in_specs=(rows, rows, rows, rows, P(), rows, rows, rows, rows, P(DP, None, CTX)),
        out_specs=(rows, rows),
        check_vma=False,
    )
```

```python
import functools
import math

import jax
import jax.numpy as jnp
from jax import lax
from jax.experimental import pallas as pl
from jax.experimental.pallas import tpu as pltpu
from jax.sharding import Mesh, PartitionSpec as P

HD = 128
CAP = 12
LOW = 8
FOLD = CAP - LOW
CTX = ("zh", "y")
DP = ("zl", "x", "c")
CHIPS = ("zh", "zl", "x")
MASKED = -1e30
F32 = jnp.float32
BF16 = jnp.bfloat16
VMEM = pl.BlockSpec(memory_space=pltpu.VMEM)
SMEM = pl.BlockSpec(memory_space=pltpu.SMEM)


def pack_kernel(gate_ref, up_ref, down_ref, out_ref):
    rows, units = gate_ref.shape
    out_ref[:, :units] = gate_ref[...]
    out_ref[:, units : 2 * units] = up_ref[...]
    for j in range(units // rows):
        out_ref[:, (2 * units + j * rows) : (2 * units + (j + 1) * rows)] = down_ref[j * rows : (j + 1) * rows, :]


def natural_block(place, cores, ring):
    return (place % cores) * ring + place // cores


def dispatch_kernel(halves, cores, ring, owners, x_ref, gain_ref, ids_ref, gates_ref, out_ref, mix_a_ref, mix_b_ref):
    tokens, width = x_ref.shape
    slots = owners * LOW
    half = width // 2
    x = x_ref[...].astype(F32)
    normed = (x * lax.rsqrt(jnp.mean(x * x, axis=-1, keepdims=True) + 1e-06) * gain_ref[...]).astype(BF16)
    step = width // (cores * ring)
    pieces = []
    for place in range(cores * ring):
        start = natural_block(place, cores, ring) * step
        pieces.append(normed[:, start : start + step])
    normed = jnp.concatenate(pieces, axis=1)

    lane = lax.broadcasted_iota(jnp.int32, (tokens, slots), 1)
    chip = lane // LOW
    per_half = owners // halves
    expert = chip % per_half * halves + chip // per_half
    place = lane % LOW
    ids = ids_ref[...]
    gates = gates_ref[...]
    hot = jnp.zeros((tokens, slots), F32)
    gate = jnp.zeros((tokens, slots), F32)
    for k in range(ids.shape[1]):
        hit = ids[:, k : k + 1] == expert
        hot = jnp.where(hit, 1.0, hot)
        gate = jnp.where(hit, gates[:, k : k + 1], gate)
    row = lax.broadcasted_iota(jnp.int32, (tokens, tokens), 0)
    col = lax.broadcasted_iota(jnp.int32, (tokens, tokens), 1)
    earlier = jnp.where(col < row, 1.0, 0.0).astype(BF16)
    rank = jnp.dot(earlier, hot.astype(BF16), preferred_element_type=F32)
    rank = jnp.where(hot > 0.5, rank, -1.0)
    in_a = rank == place.astype(F32)
    in_b = rank == (LOW + place % FOLD).astype(F32)
    in_lo = in_b & (place < FOLD)
    in_hi = in_b & (place >= FOLD)

    def put(chosen):
        return jnp.where(chosen, 1.0, 0.0).astype(BF16)

    contract = (((0,), (0,)), ((), ()))
    out_ref[:, :width] = lax.dot_general(put(in_a), normed, contract, preferred_element_type=F32).astype(BF16)
    pick = jnp.concatenate([put(in_lo), put(in_hi)], axis=0)
    stacked = jnp.concatenate([normed[:, :half], normed[:, half:]], axis=0)
    out_ref[:, width:] = lax.dot_general(pick, stacked, contract, preferred_element_type=F32).astype(BF16)

    top = gate.astype(BF16).astype(F32)
    rest = gate - top

    def mix(chosen):
        return jnp.concatenate(
            [jnp.where(chosen, top, 0.0).astype(BF16), jnp.where(chosen, rest, 0.0).astype(BF16)], axis=0
        )

    mix_a_ref[...] = mix(in_a)
    mix_b_ref[:, :slots] = mix(in_lo)
    mix_b_ref[:, slots:] = mix(in_hi)


def expert_kernel(hidden_units, x_ref, w_ref, out_ref):
    rows, cols = x_ref.shape
    width = w_ref.shape[0] * w_ref.shape[1]
    half = width // 2
    both = 2 * hidden_units
    block = w_ref.shape[1]
    count = w_ref.shape[0]

    def part(lo, hi):
        return w_ref[lo:hi, :, :both].reshape((hi - lo) * block, both)

    low_w = part(0, count // 2)
    high_w = part(count // 2, count)
    sums_a = jnp.dot(x_ref[:, :half], low_w, preferred_element_type=F32)
    sums_a = sums_a + jnp.dot(x_ref[:, half:width], high_w, preferred_element_type=F32)
    folded = x_ref[:, width:]
    first = lax.broadcasted_iota(jnp.int32, (rows, both), 0) % LOW < FOLD
    sums_b = jnp.where(
        first,
        jnp.dot(folded, low_w, preferred_element_type=F32),
        jnp.dot(folded, high_w, preferred_element_type=F32),
    )
    groups = sums_b.reshape(rows // LOW, LOW, both)
    sums_b = (groups + pltpu.roll(groups, FOLD, 1)).reshape(rows, both)

    def activate(sums):
        gate = sums[:, :hidden_units]
        return (gate / (1.0 + jnp.exp(-gate)) * sums[:, hidden_units:]).astype(BF16)

    hidden_a = activate(sums_a)
    hidden_b = activate(sums_b)

    def down(place):
        pieces = [w_ref[place, :, both + j * block : both + (j + 1) * block] for j in range(hidden_units // block)]
        return jnp.concatenate(pieces, axis=0)

    first_out = lax.broadcasted_iota(jnp.int32, (rows, 2 * block), 0) % LOW < FOLD
    for pair in range(count // 4):
        lo, hi = 2 * pair, count // 2 + 2 * pair
        low_d = jnp.concatenate([down(lo), down(lo + 1)], axis=1)
        high_d = jnp.concatenate([down(hi), down(hi + 1)], axis=1)
        out_ref[:, lo * block : (lo + 2) * block] = jnp.dot(
            hidden_a, low_d, preferred_element_type=F32
        ).astype(BF16)
        out_ref[:, hi * block : (hi + 2) * block] = jnp.dot(
            hidden_a, high_d, preferred_element_type=F32
        ).astype(BF16)
        out_ref[:, width + lo * block : width + (lo + 2) * block] = jnp.where(
            first_out,
            jnp.dot(hidden_b, low_d, preferred_element_type=F32),
            jnp.dot(hidden_b, high_d, preferred_element_type=F32),
        ).astype(BF16)


def combine_kernel(cores, ring, back_ref, mix_a_ref, mix_b_ref, out_ref):
    tokens, width = out_ref.shape
    half = width // 2
    slots = back_ref.shape[0]
    step = width // (cores * ring)
    folded = back_ref[:, width:]
    for side in range(2):
        both = jnp.dot(
            mix_a_ref[...], back_ref[:, side * half : (side + 1) * half], preferred_element_type=F32
        ) + jnp.dot(
            mix_b_ref[:, side * slots : (side + 1) * slots], folded, preferred_element_type=F32
        )
        total = (both[:tokens] + both[tokens:]).astype(BF16)
        for i in range(half // step):
            start = natural_block(side * (half // step) + i, cores, ring) * step
            out_ref[:, start : start + step] = total[:, i * step : (i + 1) * step]


def attend_kernel(halves, ring, heads_kv, q_ref, kv_ref, place_ref, out_ref):
    tokens, wide = q_ref.shape
    heads = wide // HD
    group = heads // heads_kv
    blocks = kv_ref.shape[0]
    keys = blocks * kv_ref.shape[1]
    scale = 1.0 / math.sqrt(HD)
    lane = lax.broadcasted_iota(jnp.int32, (tokens, keys), 1)
    row = lax.broadcasted_iota(jnp.int32, (tokens, keys), 0)
    block = lane // tokens
    here = place_ref[0] // ring
    passed = jnp.where(here == 0, halves, 0)
    side = jnp.where(block % halves == 0, here, passed)
    key_pos = (side * ring + block // halves) * tokens + lane % tokens
    allowed = key_pos <= row + place_ref[0] * tokens
    for g in range(heads_kv):
        key = kv_ref[:, :, g * HD : (g + 1) * HD].reshape(keys, HD)
        value = kv_ref[:, :, (heads_kv + g) * HD : (heads_kv + g + 1) * HD].reshape(keys, HD)

        @pl.loop(0, group)
        def _(i):
            at = pl.ds(pl.multiple_of((g * group + i) * HD, HD), HD)
            scores = lax.dot_general(
                q_ref[:, at], key, (((1,), (1,)), ((), ())), preferred_element_type=F32
            )
            scores = jnp.where(allowed, scores * scale, MASKED)
            largest = jnp.max(scores, axis=-1, keepdims=True)
            probs = jnp.exp(scores - largest)
            total = jnp.sum(probs, axis=-1, keepdims=True)
            mixed = jnp.dot(probs.astype(BF16), value, preferred_element_type=F32)
            out_ref[:, at] = (mixed / total).astype(BF16)


def estimate(flops, bytes_accessed, transcendentals=0):
    return pl.CostEstimate(flops=flops, bytes_accessed=bytes_accessed, transcendentals=transcendentals)


def shards(
    queries, key_rows, value_rows, stream, norm_gain, expert_ids, gate_values, w_gate, w_up, w_down
):
    tokens, width = stream.shape[1:]
    heads_kv = key_rows.shape[2] // HD
    hidden_units = w_gate.shape[2]
    halves, ring, cores = lax.axis_size("zh"), lax.axis_size("y"), lax.axis_size("c")
    owners = lax.axis_size(DP)
    slots = owners * LOW
    wide = width + width // 2
    params = pltpu.CompilerParams(vmem_limit_bytes=48 * 1024 * 1024)

    with jax.named_scope("weights"):
        packed = pl.pallas_call(
            pack_kernel,
            out_shape=jax.ShapeDtypeStruct((w_gate.shape[1], 3 * hidden_units), BF16),
            in_specs=[VMEM] * 3,
            out_specs=VMEM,
            name="pack",
        )(w_gate[0], w_up[0], w_down[0])
        swap = [(h * cores + c, c * cores + h) for h in range(halves) for c in range(cores)]
        part = lax.ppermute(packed, ("zh", "c"), swap)
    with jax.named_scope("dispatch"):
        ids, _ = lax.optimization_barrier((expert_ids[0], packed))
        outgoing, mix_a, mix_b = pl.pallas_call(
            functools.partial(dispatch_kernel, halves, cores, ring, owners),
            out_shape=(
                jax.ShapeDtypeStruct((slots, wide), BF16),
                jax.ShapeDtypeStruct((2 * tokens, slots), BF16),
                jax.ShapeDtypeStruct((2 * tokens, 2 * slots), BF16),
            ),
            in_specs=[VMEM] * 4,
            out_specs=(VMEM,) * 3,
            compiler_params=params,
            cost_estimate=estimate(4 * 256 * 256 * 2048, 4 * 1024 * 1024),
            name="dispatch",
        )(stream[0], norm_gain[None, :], ids, gate_values[0])
        part, outgoing = lax.optimization_barrier((part, outgoing))
        weights = lax.all_gather(part, ("y", "c"), axis=0)
        arrived = lax.all_to_all(
            outgoing.reshape(owners, LOW, wide), CHIPS, split_axis=0, concat_axis=0, tiled=True
        ).reshape(slots, wide)

    with jax.named_scope("keys"):
        key_local, value_local, outgoing, part = lax.optimization_barrier(
            (key_rows[0], value_rows[0], outgoing, part)
        )
        kv = jnp.concatenate([key_local, value_local], axis=1)
        kv_passed = lax.ppermute(kv, "zh", [(0, 1)])
        kv_pair = jnp.stack([kv, kv_passed])
        kv_all = lax.all_gather(kv_pair, "y", axis=0, tiled=True)
        arrived, kv_pair = lax.optimization_barrier((arrived, kv_pair))

    with jax.named_scope("experts"):
        answers = pl.pallas_call(
            functools.partial(expert_kernel, hidden_units),
            out_shape=jax.ShapeDtypeStruct((slots, wide), BF16),
            in_specs=[VMEM, VMEM],
            out_specs=VMEM,
            compiler_params=params,
            cost_estimate=estimate(6 * 512 * 2048 * 384, 8 * 1024 * 1024),
            name="experts",
        )(arrived, weights)
        returned = lax.all_to_all(
            answers.reshape(owners, LOW, wide), CHIPS, split_axis=0, concat_axis=0, tiled=True
        ).reshape(slots, wide)

    with jax.named_scope("attend"):
        place = lax.axis_index(CTX).astype(jnp.int32)[None]
        attended = pl.pallas_call(
            functools.partial(attend_kernel, halves, ring, heads_kv),
            out_shape=jax.ShapeDtypeStruct(queries.shape[1:], BF16),
            in_specs=[VMEM, VMEM, SMEM],
            out_specs=VMEM,
            compiler_params=params,
            cost_estimate=estimate(4 * 2048 * 128 * 2048, 4 * 1024 * 1024, 16 * 128 * 2048),
            name="attend",
        )(queries[0], kv_all, place)

    with jax.named_scope("combine"):
        expert_out = pl.pallas_call(
            functools.partial(combine_kernel, cores, ring),
            out_shape=jax.ShapeDtypeStruct((tokens, width), BF16),
            in_specs=[VMEM] * 3,
            out_specs=VMEM,
            compiler_params=params,
            cost_estimate=estimate(2 * 256 * 512 * 2048, 3 * 1024 * 1024),
            name="combine",
        )(returned, mix_a, mix_b)
    return (attended[None], expert_out[None])


def solution(mesh):
    fine = Mesh(mesh.devices.reshape(2, 8, 4, 4, 2), CTX + DP)
    rows = P(DP, CTX, None)
    return jax.shard_map(
        shards,
        mesh=fine,
        in_specs=(rows, rows, rows, rows, P(), rows, rows, rows, rows, P(DP, None, CTX)),
        out_specs=(rows, rows),
        check_vma=False,
    )
```

```python
import functools
import math

import jax
import jax.numpy as jnp
from jax import lax
from jax.experimental import pallas as pl
from jax.experimental.pallas import tpu as pltpu
from jax.sharding import Mesh, PartitionSpec as P

HD = 128
CAP = 12
LOW = 8
FOLD = CAP - LOW
CTX = ("zh", "y")
DP = ("zl", "x", "c")
CHIPS = ("zh", "zl", "x")
MASKED = -1e30
F32 = jnp.float32
BF16 = jnp.bfloat16
VMEM = pl.BlockSpec(memory_space=pltpu.VMEM)
HBM = pl.BlockSpec(memory_space=pltpu.HBM)
SMEM = pl.BlockSpec(memory_space=pltpu.SMEM)


def pack_kernel(gate_ref, up_ref, down_ref, out_ref):
    rows, units = gate_ref.shape
    out_ref[:, :units] = gate_ref[...]
    out_ref[:, units : 2 * units] = up_ref[...]
    for j in range(units // rows):
        out_ref[:, (2 * units + j * rows) : (2 * units + (j + 1) * rows)] = down_ref[j * rows : (j + 1) * rows, :]


def natural_block(place, cores, ring):
    return (place % cores) * ring + place // cores


def dispatch_kernel(halves, cores, ring, owners, x_ref, gain_ref, ids_ref, gates_ref, out_ref, mix_a_ref, mix_b_ref):
    tokens, width = x_ref.shape
    slots = owners * LOW
    half = width // 2
    x = x_ref[...].astype(F32)
    normed = (x * lax.rsqrt(jnp.mean(x * x, axis=-1, keepdims=True) + 1e-06) * gain_ref[...]).astype(BF16)
    step = width // (cores * ring)
    pieces = []
    for place in range(cores * ring):
        start = natural_block(place, cores, ring) * step
        pieces.append(normed[:, start : start + step])
    normed = jnp.concatenate(pieces, axis=1)

    lane = lax.broadcasted_iota(jnp.int32, (tokens, slots), 1)
    chip = lane // LOW
    per_half = owners // halves
    expert = chip % per_half * halves + chip // per_half
    place = lane % LOW
    ids = ids_ref[...]
    gates = gates_ref[...]
    hot = jnp.zeros((tokens, slots), F32)
    gate = jnp.zeros((tokens, slots), F32)
    for k in range(ids.shape[1]):
        hit = ids[:, k : k + 1] == expert
        hot = jnp.where(hit, 1.0, hot)
        gate = jnp.where(hit, gates[:, k : k + 1], gate)
    row = lax.broadcasted_iota(jnp.int32, (tokens, tokens), 0)
    col = lax.broadcasted_iota(jnp.int32, (tokens, tokens), 1)
    earlier = jnp.where(col < row, 1.0, 0.0).astype(BF16)
    rank = jnp.dot(earlier, hot.astype(BF16), preferred_element_type=F32)
    rank = jnp.where(hot > 0.5, rank, -1.0)
    in_a = rank == place.astype(F32)
    in_b = rank == (LOW + place % FOLD).astype(F32)
    in_lo = in_b & (place < FOLD)
    in_hi = in_b & (place >= FOLD)

    def put(chosen):
        return jnp.where(chosen, 1.0, 0.0).astype(BF16)

    contract = (((0,), (0,)), ((), ()))
    out_ref[:, :width] = lax.dot_general(put(in_a), normed, contract, preferred_element_type=F32).astype(BF16)
    pick = jnp.concatenate([put(in_lo), put(in_hi)], axis=0)
    stacked = jnp.concatenate([normed[:, :half], normed[:, half:]], axis=0)
    out_ref[:, width:] = lax.dot_general(pick, stacked, contract, preferred_element_type=F32).astype(BF16)

    top = gate.astype(BF16).astype(F32)
    rest = gate - top

    def mix(chosen):
        return jnp.concatenate(
            [jnp.where(chosen, top, 0.0).astype(BF16), jnp.where(chosen, rest, 0.0).astype(BF16)], axis=0
        )

    mix_a_ref[...] = mix(in_a)
    mix_b_ref[:, :slots] = mix(in_lo)
    mix_b_ref[:, slots:] = mix(in_hi)


def expert_kernel(hidden_units, x_ref, w_hbm, out_ref, w_ref, sems):
    rows, cols = x_ref.shape
    width = w_ref.shape[0] * w_ref.shape[1]
    half = width // 2
    both = 2 * hidden_units
    block = w_ref.shape[1]
    count = w_ref.shape[0]

    chunks = sems.shape[0]
    per = count // chunks
    copies = []
    for i in range(chunks):
        at = pl.ds(i * per, per)
        copies.append(pltpu.make_async_copy(w_hbm.at[at], w_ref.at[at], sems.at[i]))
        copies[-1].start()
    sums_a, folds = None, [None, None]
    for i in range(chunks):
        copies[i].wait()
        piece = w_ref[i * per : (i + 1) * per, :, :both].reshape(per * block, both)
        start, side = i * per * block, 2 * i // chunks
        more = jnp.dot(x_ref[:, start : start + per * block], piece, preferred_element_type=F32)
        sums_a = more if sums_a is None else sums_a + more
        start = width + start - side * half
        more = jnp.dot(x_ref[:, start : start + per * block], piece, preferred_element_type=F32)
        folds[side] = more if folds[side] is None else folds[side] + more
    first = lax.broadcasted_iota(jnp.int32, (rows, both), 0) % LOW < FOLD
    sums_b = jnp.where(first, folds[0], folds[1])
    groups = sums_b.reshape(rows // LOW, LOW, both)
    sums_b = (groups + pltpu.roll(groups, FOLD, 1)).reshape(rows, both)

    def activate(sums):
        gate = sums[:, :hidden_units]
        return (gate / (1.0 + jnp.exp(-gate)) * sums[:, hidden_units:]).astype(BF16)

    hidden_a = activate(sums_a)
    hidden_b = activate(sums_b)

    def down(place):
        pieces = [w_ref[place, :, both + j * block : both + (j + 1) * block] for j in range(hidden_units // block)]
        return jnp.concatenate(pieces, axis=0)

    first_out = lax.broadcasted_iota(jnp.int32, (rows, 2 * block), 0) % LOW < FOLD
    for pair in range(count // 4):
        lo, hi = 2 * pair, count // 2 + 2 * pair
        low_d = jnp.concatenate([down(lo), down(lo + 1)], axis=1)
        high_d = jnp.concatenate([down(hi), down(hi + 1)], axis=1)
        out_ref[:, lo * block : (lo + 2) * block] = jnp.dot(
            hidden_a, low_d, preferred_element_type=F32
        ).astype(BF16)
        out_ref[:, hi * block : (hi + 2) * block] = jnp.dot(
            hidden_a, high_d, preferred_element_type=F32
        ).astype(BF16)
        out_ref[:, width + lo * block : width + (lo + 2) * block] = jnp.where(
            first_out,
            jnp.dot(hidden_b, low_d, preferred_element_type=F32),
            jnp.dot(hidden_b, high_d, preferred_element_type=F32),
        ).astype(BF16)


def combine_kernel(cores, ring, back_ref, mix_a_ref, mix_b_ref, out_ref):
    tokens, width = out_ref.shape
    half = width // 2
    slots = back_ref.shape[0]
    step = width // (cores * ring)
    folded = back_ref[:, width:]
    for side in range(2):
        both = jnp.dot(
            mix_a_ref[...], back_ref[:, side * half : (side + 1) * half], preferred_element_type=F32
        ) + jnp.dot(
            mix_b_ref[:, side * slots : (side + 1) * slots], folded, preferred_element_type=F32
        )
        total = (both[:tokens] + both[tokens:]).astype(BF16)
        for i in range(half // step):
            start = natural_block(side * (half // step) + i, cores, ring) * step
            out_ref[:, start : start + step] = total[:, i * step : (i + 1) * step]


def attend_kernel(halves, ring, heads_kv, q_ref, kv_hbm, place_ref, out_ref, kv_ref, sem):
    tokens, wide = q_ref.shape
    group = wide // HD // heads_kv
    blocks = halves * ring
    keys = blocks * tokens
    factor = math.log2(math.e) / math.sqrt(HD)
    copy = pltpu.make_async_copy(kv_hbm, kv_ref, sem)
    copy.start()
    lane = lax.broadcasted_iota(jnp.int32, (tokens, keys), 1)
    row = lax.broadcasted_iota(jnp.int32, (tokens, keys), 0)
    block = lane // tokens
    here = place_ref[0] // ring
    passed = jnp.where(here == 0, halves, 0)
    side = jnp.where(block % halves == 0, here, passed)
    key_pos = (side * ring + block // halves) * tokens + lane % tokens
    bias = jnp.where(key_pos <= row + place_ref[0] * tokens, 0.0, MASKED)
    ones = jnp.ones((keys, HD), BF16)
    copy.wait()
    for g in range(heads_kv):
        key = kv_ref[:, :, g * HD : (g + 1) * HD].reshape(keys, HD)
        value = kv_ref[:, :, (heads_kv + g) * HD : (heads_kv + g + 1) * HD].reshape(keys, HD)
        value = jnp.concatenate([value, ones], axis=1)
        for i in range(g * group, (g + 1) * group):
            at = slice(i * HD, (i + 1) * HD)
            scores = lax.dot_general(
                q_ref[:, at], key, (((1,), (1,)), ((), ())), preferred_element_type=F32
            )
            scores = scores * factor + bias
            probs = jnp.exp2(scores - jnp.max(scores, axis=-1, keepdims=True))
            mixed = jnp.dot(probs.astype(BF16), value, preferred_element_type=F32)
            out_ref[:, at] = (mixed[:, :HD] / mixed[:, HD:]).astype(BF16)


def estimate(flops, bytes_accessed, transcendentals=0):
    return pl.CostEstimate(flops=flops, bytes_accessed=bytes_accessed, transcendentals=transcendentals)


def shards(
    queries, key_rows, value_rows, stream, norm_gain, expert_ids, gate_values, w_gate, w_up, w_down
):
    tokens, width = stream.shape[1:]
    heads_kv = key_rows.shape[2] // HD
    hidden_units = w_gate.shape[2]
    halves, ring, cores = lax.axis_size("zh"), lax.axis_size("y"), lax.axis_size("c")
    owners = lax.axis_size(DP)
    slots = owners * LOW
    wide = width + width // 2
    params = pltpu.CompilerParams(vmem_limit_bytes=48 * 1024 * 1024)

    with jax.named_scope("weights"):
        packed = pl.pallas_call(
            pack_kernel,
            out_shape=jax.ShapeDtypeStruct((w_gate.shape[1], 3 * hidden_units), BF16),
            in_specs=[VMEM] * 3,
            out_specs=VMEM,
            name="pack",
        )(w_gate[0], w_up[0], w_down[0])
        swap = [(h * cores + c, c * cores + h) for h in range(halves) for c in range(cores)]
        part = lax.ppermute(packed, ("zh", "c"), swap)
    with jax.named_scope("dispatch"):
        ids, _ = lax.optimization_barrier((expert_ids[0], packed))
        outgoing, mix_a, mix_b = pl.pallas_call(
            functools.partial(dispatch_kernel, halves, cores, ring, owners),
            out_shape=(
                jax.ShapeDtypeStruct((slots, wide), BF16),
                jax.ShapeDtypeStruct((2 * tokens, slots), BF16),
                jax.ShapeDtypeStruct((2 * tokens, 2 * slots), BF16),
            ),
            in_specs=[VMEM] * 4,
            out_specs=(VMEM,) * 3,
            compiler_params=params,
            cost_estimate=estimate(4 * 256 * 256 * 2048, 4 * 1024 * 1024),
            name="dispatch",
        )(stream[0], norm_gain[None, :], ids, gate_values[0])
        part, outgoing = lax.optimization_barrier((part, outgoing))
        weights = lax.all_gather(part, ("y", "c"), axis=0)
        arrived = lax.all_to_all(
            outgoing.reshape(owners, LOW, wide), CHIPS, split_axis=0, concat_axis=0, tiled=True
        ).reshape(slots, wide)

    with jax.named_scope("keys"):
        key_local, value_local, outgoing, part = lax.optimization_barrier(
            (key_rows[0], value_rows[0], outgoing, part)
        )
        kv = jnp.concatenate([key_local, value_local], axis=1)
        kv_passed = lax.ppermute(kv, "zh", [(0, 1)])
        kv_pair = jnp.stack([kv, kv_passed])
        kv_all = lax.all_gather(kv_pair, "y", axis=0, tiled=True)
        arrived, kv_pair = lax.optimization_barrier((arrived, kv_pair))

    with jax.named_scope("experts"):
        answers = pl.pallas_call(
            functools.partial(expert_kernel, hidden_units),
            out_shape=jax.ShapeDtypeStruct((slots, wide), BF16),
            in_specs=[VMEM, HBM],
            out_specs=VMEM,
            scratch_shapes=[pltpu.VMEM(weights.shape, BF16), pltpu.SemaphoreType.DMA((4,))],
            compiler_params=params,
            cost_estimate=estimate(6 * 512 * 2048 * 384, 8 * 1024 * 1024),
            name="experts",
        )(arrived, weights)
        returned = lax.all_to_all(
            answers.reshape(owners, LOW, wide), CHIPS, split_axis=0, concat_axis=0, tiled=True
        ).reshape(slots, wide)

    with jax.named_scope("attend"):
        place = lax.axis_index(CTX).astype(jnp.int32)[None]
        attended = pl.pallas_call(
            functools.partial(attend_kernel, halves, ring, heads_kv),
            out_shape=jax.ShapeDtypeStruct(queries.shape[1:], BF16),
            in_specs=[VMEM, HBM, SMEM],
            out_specs=VMEM,
            scratch_shapes=[
                pltpu.VMEM((halves * ring, tokens, 2 * heads_kv * HD), BF16),
                pltpu.SemaphoreType.DMA,
            ],
            compiler_params=pltpu.CompilerParams(vmem_limit_bytes=60 * 1024 * 1024),
            cost_estimate=estimate(4 * 2048 * 128 * 2048, 4 * 1024 * 1024, 16 * 128 * 2048),
            name="attend",
        )(queries[0], kv_all, place)

    with jax.named_scope("combine"):
        expert_out = pl.pallas_call(
            functools.partial(combine_kernel, cores, ring),
            out_shape=jax.ShapeDtypeStruct((tokens, width), BF16),
            in_specs=[VMEM] * 3,
            out_specs=VMEM,
            compiler_params=params,
            cost_estimate=estimate(2 * 256 * 512 * 2048, 3 * 1024 * 1024),
            name="combine",
        )(returned, mix_a, mix_b)
    return (attended[None], expert_out[None])


def solution(mesh):
    fine = Mesh(mesh.devices.reshape(2, 8, 4, 4, 2), CTX + DP)
    rows = P(DP, CTX, None)
    return jax.shard_map(
        shards,
        mesh=fine,
        in_specs=(rows, rows, rows, rows, P(), rows, rows, rows, rows, P(DP, None, CTX)),
        out_specs=(rows, rows),
        check_vma=False,
    )
```

```python
import functools
import math

import jax
import jax.numpy as jnp
from jax import lax
from jax.experimental import pallas as pl
from jax.experimental.pallas import tpu as pltpu
from jax.sharding import Mesh, PartitionSpec as P

HD = 128
CAP = 12
LOW = 8
FOLD = CAP - LOW
CTX = ("zh", "y")
DP = ("zl", "x", "c")
CHIPS = ("zh", "zl", "x")
MASKED = -1e30
F32 = jnp.float32
BF16 = jnp.bfloat16
VMEM = pl.BlockSpec(memory_space=pltpu.VMEM)
HBM = pl.BlockSpec(memory_space=pltpu.HBM)
SMEM = pl.BlockSpec(memory_space=pltpu.SMEM)


def pack_kernel(gate_ref, up_ref, down_ref, out_ref):
    rows, units = gate_ref.shape
    out_ref[:, :units] = gate_ref[...]
    out_ref[:, units : 2 * units] = up_ref[...]
    for j in range(units // rows):
        out_ref[:, (2 * units + j * rows) : (2 * units + (j + 1) * rows)] = down_ref[j * rows : (j + 1) * rows, :]


def host_place(z, core, depth, halves):
    return (z + depth // 2 + core * depth) % (depth * halves)


def natural_block(place, cores, ring):
    return (place % cores) * ring + place // cores


def dispatch_kernel(halves, depth, cores, ring, owners, x_ref, gain_ref, ids_ref, gates_ref, out_ref, mix_a_ref, mix_b_ref):
    tokens, width = x_ref.shape
    slots = owners * LOW
    half = width // 2
    x = x_ref[...].astype(F32)
    normed = (x * lax.rsqrt(jnp.mean(x * x, axis=-1, keepdims=True) + 1e-06) * gain_ref[...]).astype(BF16)
    step = width // (cores * ring)
    pieces = []
    for place in range(cores * ring):
        start = natural_block(place, cores, ring) * step
        pieces.append(normed[:, start : start + step])
    normed = jnp.concatenate(pieces, axis=1)

    lane = lax.broadcasted_iota(jnp.int32, (tokens, slots), 1)
    chip = lane // LOW
    across = owners // (halves * depth)
    turn = (chip // across + halves * depth - depth // 2) % (halves * depth)
    expert = (turn % depth * across + chip % across) * cores + turn // depth
    place = lane % LOW
    ids = ids_ref[...]
    gates = gates_ref[...]
    hot = jnp.zeros((tokens, slots), F32)
    gate = jnp.zeros((tokens, slots), F32)
    for k in range(ids.shape[1]):
        hit = ids[:, k : k + 1] == expert
        hot = jnp.where(hit, 1.0, hot)
        gate = jnp.where(hit, gates[:, k : k + 1], gate)
    row = lax.broadcasted_iota(jnp.int32, (tokens, tokens), 0)
    col = lax.broadcasted_iota(jnp.int32, (tokens, tokens), 1)
    earlier = jnp.where(col < row, 1.0, 0.0).astype(BF16)
    rank = jnp.dot(earlier, hot.astype(BF16), preferred_element_type=F32)
    rank = jnp.where(hot > 0.5, rank, -1.0)
    in_a = rank == place.astype(F32)
    in_b = rank == (LOW + place % FOLD).astype(F32)
    in_lo = in_b & (place < FOLD)
    in_hi = in_b & (place >= FOLD)

    def put(chosen):
        return jnp.where(chosen, 1.0, 0.0).astype(BF16)

    contract = (((0,), (0,)), ((), ()))
    out_ref[:, :width] = lax.dot_general(put(in_a), normed, contract, preferred_element_type=F32).astype(BF16)
    pick = jnp.concatenate([put(in_lo), put(in_hi)], axis=0)
    stacked = jnp.concatenate([normed[:, :half], normed[:, half:]], axis=0)
    out_ref[:, width:] = lax.dot_general(pick, stacked, contract, preferred_element_type=F32).astype(BF16)

    top = gate.astype(BF16).astype(F32)
    rest = gate - top

    def mix(chosen):
        return jnp.concatenate(
            [jnp.where(chosen, top, 0.0).astype(BF16), jnp.where(chosen, rest, 0.0).astype(BF16)], axis=0
        )

    mix_a_ref[...] = mix(in_a)
    mix_b_ref[:, :slots] = mix(in_lo)
    mix_b_ref[:, slots:] = mix(in_hi)


def expert_kernel(hidden_units, x_ref, w_hbm, out_ref, w_ref, sems):
    rows, cols = x_ref.shape
    width = w_ref.shape[0] * w_ref.shape[1]
    half = width // 2
    both = 2 * hidden_units
    block = w_ref.shape[1]
    count = w_ref.shape[0]

    chunks = sems.shape[0]
    per = count // chunks
    copies = []
    for i in range(chunks):
        at = pl.ds(i * per, per)
        copies.append(pltpu.make_async_copy(w_hbm.at[at], w_ref.at[at], sems.at[i]))
        copies[-1].start()
    sums_a, folds = None, [None, None]
    for i in range(chunks):
        copies[i].wait()
        piece = w_ref[i * per : (i + 1) * per, :, :both].reshape(per * block, both)
        start, side = i * per * block, 2 * i // chunks
        more = jnp.dot(x_ref[:, start : start + per * block], piece, preferred_element_type=F32)
        sums_a = more if sums_a is None else sums_a + more
        start = width + start - side * half
        more = jnp.dot(x_ref[:, start : start + per * block], piece, preferred_element_type=F32)
        folds[side] = more if folds[side] is None else folds[side] + more
    first = lax.broadcasted_iota(jnp.int32, (rows, both), 0) % LOW < FOLD
    sums_b = jnp.where(first, folds[0], folds[1])
    groups = sums_b.reshape(rows // LOW, LOW, both)
    sums_b = (groups + pltpu.roll(groups, FOLD, 1)).reshape(rows, both)

    def activate(sums):
        gate = sums[:, :hidden_units]
        return (gate / (1.0 + jnp.exp(-gate)) * sums[:, hidden_units:]).astype(BF16)

    hidden_a = activate(sums_a)
    hidden_b = activate(sums_b)

    def down(place):
        pieces = [w_ref[place, :, both + j * block : both + (j + 1) * block] for j in range(hidden_units // block)]
        return jnp.concatenate(pieces, axis=0)

    first_out = lax.broadcasted_iota(jnp.int32, (rows, 2 * block), 0) % LOW < FOLD
    for pair in range(count // 4):
        lo, hi = 2 * pair, count // 2 + 2 * pair
        low_d = jnp.concatenate([down(lo), down(lo + 1)], axis=1)
        high_d = jnp.concatenate([down(hi), down(hi + 1)], axis=1)
        out_ref[:, lo * block : (lo + 2) * block] = jnp.dot(
            hidden_a, low_d, preferred_element_type=F32
        ).astype(BF16)
        out_ref[:, hi * block : (hi + 2) * block] = jnp.dot(
            hidden_a, high_d, preferred_element_type=F32
        ).astype(BF16)
        out_ref[:, width + lo * block : width + (lo + 2) * block] = jnp.where(
            first_out,
            jnp.dot(hidden_b, low_d, preferred_element_type=F32),
            jnp.dot(hidden_b, high_d, preferred_element_type=F32),
        ).astype(BF16)


def combine_kernel(cores, ring, back_ref, mix_a_ref, mix_b_ref, out_ref):
    tokens, width = out_ref.shape
    half = width // 2
    slots = back_ref.shape[0]
    step = width // (cores * ring)
    folded = back_ref[:, width:]
    for side in range(2):
        both = jnp.dot(
            mix_a_ref[...], back_ref[:, side * half : (side + 1) * half], preferred_element_type=F32
        ) + jnp.dot(
            mix_b_ref[:, side * slots : (side + 1) * slots], folded, preferred_element_type=F32
        )
        total = (both[:tokens] + both[tokens:]).astype(BF16)
        for i in range(half // step):
            start = natural_block(side * (half // step) + i, cores, ring) * step
            out_ref[:, start : start + step] = total[:, i * step : (i + 1) * step]


def attend_kernel(halves, ring, heads_kv, q_ref, kv_hbm, place_ref, out_ref, kv_ref, sem):
    tokens, wide = q_ref.shape
    group = wide // HD // heads_kv
    blocks = halves * ring
    keys = blocks * tokens
    factor = math.log2(math.e) / math.sqrt(HD)
    copy = pltpu.make_async_copy(kv_hbm, kv_ref, sem)
    copy.start()
    lane = lax.broadcasted_iota(jnp.int32, (tokens, keys), 1)
    row = lax.broadcasted_iota(jnp.int32, (tokens, keys), 0)
    block = lane // tokens
    here = place_ref[0] // ring
    passed = jnp.where(here == 0, halves, 0)
    side = jnp.where(block % halves == 0, here, passed)
    key_pos = (side * ring + block // halves) * tokens + lane % tokens
    bias = jnp.where(key_pos <= row + place_ref[0] * tokens, 0.0, MASKED)
    ones = jnp.ones((keys, HD), BF16)
    copy.wait()
    for g in range(heads_kv):
        key = kv_ref[:, :, g * HD : (g + 1) * HD].reshape(keys, HD)
        value = kv_ref[:, :, (heads_kv + g) * HD : (heads_kv + g + 1) * HD].reshape(keys, HD)
        value = jnp.concatenate([value, ones], axis=1)
        for i in range(g * group, (g + 1) * group):
            at = slice(i * HD, (i + 1) * HD)
            scores = lax.dot_general(
                q_ref[:, at], key, (((1,), (1,)), ((), ())), preferred_element_type=F32
            )
            scores = scores * factor + bias
            probs = jnp.exp2(scores - jnp.max(scores, axis=-1, keepdims=True))
            mixed = jnp.dot(probs.astype(BF16), value, preferred_element_type=F32)
            out_ref[:, at] = (mixed[:, :HD] / mixed[:, HD:]).astype(BF16)


def estimate(flops, bytes_accessed, transcendentals=0):
    return pl.CostEstimate(flops=flops, bytes_accessed=bytes_accessed, transcendentals=transcendentals)


def shards(
    queries, key_rows, value_rows, stream, norm_gain, expert_ids, gate_values, w_gate, w_up, w_down
):
    tokens, width = stream.shape[1:]
    heads_kv = key_rows.shape[2] // HD
    hidden_units = w_gate.shape[2]
    halves, ring, cores = lax.axis_size("zh"), lax.axis_size("y"), lax.axis_size("c")
    depth = lax.axis_size("zl")
    owners = lax.axis_size(DP)
    slots = owners * LOW
    wide = width + width // 2
    params = pltpu.CompilerParams(vmem_limit_bytes=48 * 1024 * 1024)

    with jax.named_scope("weights"):
        packed = pl.pallas_call(
            pack_kernel,
            out_shape=jax.ShapeDtypeStruct((w_gate.shape[1], 3 * hidden_units), BF16),
            in_specs=[VMEM] * 3,
            out_specs=VMEM,
            name="pack",
        )(w_gate[0], w_up[0], w_down[0])
        route = []
        for h in range(halves):
            for z in range(depth):
                for c in range(cores):
                    to = host_place(z, c, depth, halves)
                    route.append(((h * depth + z) * cores + c, to * cores + h))
        part = lax.ppermute(packed, ("zh", "zl", "c"), route)
    with jax.named_scope("dispatch"):
        ids, _ = lax.optimization_barrier((expert_ids[0], packed))
        outgoing, mix_a, mix_b = pl.pallas_call(
            functools.partial(dispatch_kernel, halves, depth, cores, ring, owners),
            out_shape=(
                jax.ShapeDtypeStruct((slots, wide), BF16),
                jax.ShapeDtypeStruct((2 * tokens, slots), BF16),
                jax.ShapeDtypeStruct((2 * tokens, 2 * slots), BF16),
            ),
            in_specs=[VMEM] * 4,
            out_specs=(VMEM,) * 3,
            compiler_params=params,
            cost_estimate=estimate(4 * 256 * 256 * 2048, 4 * 1024 * 1024),
            name="dispatch",
        )(stream[0], norm_gain[None, :], ids, gate_values[0])
        part, outgoing = lax.optimization_barrier((part, outgoing))
        weights = lax.all_gather(part, ("y", "c"), axis=0)
        arrived = lax.all_to_all(
            outgoing.reshape(owners, LOW, wide), CHIPS, split_axis=0, concat_axis=0, tiled=True
        ).reshape(slots, wide)

    with jax.named_scope("keys"):
        key_local, value_local, outgoing, part = lax.optimization_barrier(
            (key_rows[0], value_rows[0], outgoing, part)
        )
        kv = jnp.concatenate([key_local, value_local], axis=1)
        kv_passed = lax.ppermute(kv, "zh", [(0, 1)])
        kv_pair = jnp.stack([kv, kv_passed])
        kv_all = lax.all_gather(kv_pair, "y", axis=0, tiled=True)
        arrived, kv_pair = lax.optimization_barrier((arrived, kv_pair))

    with jax.named_scope("experts"):
        answers = pl.pallas_call(
            functools.partial(expert_kernel, hidden_units),
            out_shape=jax.ShapeDtypeStruct((slots, wide), BF16),
            in_specs=[VMEM, HBM],
            out_specs=VMEM,
            scratch_shapes=[pltpu.VMEM(weights.shape, BF16), pltpu.SemaphoreType.DMA((4,))],
            compiler_params=params,
            cost_estimate=estimate(6 * 512 * 2048 * 384, 8 * 1024 * 1024),
            name="experts",
        )(arrived, weights)
        returned = lax.all_to_all(
            answers.reshape(owners, LOW, wide), CHIPS, split_axis=0, concat_axis=0, tiled=True
        ).reshape(slots, wide)

    with jax.named_scope("attend"):
        place = lax.axis_index(CTX).astype(jnp.int32)[None]
        attended = pl.pallas_call(
            functools.partial(attend_kernel, halves, ring, heads_kv),
            out_shape=jax.ShapeDtypeStruct(queries.shape[1:], BF16),
            in_specs=[VMEM, HBM, SMEM],
            out_specs=VMEM,
            scratch_shapes=[
                pltpu.VMEM((halves * ring, tokens, 2 * heads_kv * HD), BF16),
                pltpu.SemaphoreType.DMA,
            ],
            compiler_params=pltpu.CompilerParams(vmem_limit_bytes=60 * 1024 * 1024),
            cost_estimate=estimate(4 * 2048 * 128 * 2048, 4 * 1024 * 1024, 16 * 128 * 2048),
            name="attend",
        )(queries[0], kv_all, place)

    with jax.named_scope("combine"):
        expert_out = pl.pallas_call(
            functools.partial(combine_kernel, cores, ring),
            out_shape=jax.ShapeDtypeStruct((tokens, width), BF16),
            in_specs=[VMEM] * 3,
            out_specs=VMEM,
            compiler_params=params,
            cost_estimate=estimate(2 * 256 * 512 * 2048, 3 * 1024 * 1024),
            name="combine",
        )(returned, mix_a, mix_b)
    return (attended[None], expert_out[None])


def solution(mesh):
    fine = Mesh(mesh.devices.reshape(2, 8, 4, 4, 2), CTX + DP)
    rows = P(DP, CTX, None)
    return jax.shard_map(
        shards,
        mesh=fine,
        in_specs=(rows, rows, rows, rows, P(), rows, rows, rows, rows, P(DP, None, CTX)),
        out_specs=(rows, rows),
        check_vma=False,
    )
```

```python
import functools
import math

import jax
import jax.numpy as jnp
from jax import lax
from jax.experimental import pallas as pl
from jax.experimental.pallas import tpu as pltpu
from jax.sharding import Mesh, PartitionSpec as P

HD = 128
CAP = 12
LOW = 8
FOLD = CAP - LOW
CTX = ("zh", "y")
DP = ("zl", "x", "c")
CHIPS = ("zh", "zl", "x")
MASKED = -1e30
F32 = jnp.float32
BF16 = jnp.bfloat16
VMEM = pl.BlockSpec(memory_space=pltpu.VMEM)
HBM = pl.BlockSpec(memory_space=pltpu.HBM)
SMEM = pl.BlockSpec(memory_space=pltpu.SMEM)


def pack_kernel(gate_ref, up_ref, down_ref, out_ref, sems):
    rows, units = gate_ref.shape
    copies = [
        pltpu.make_async_copy(gate_ref, out_ref.at[:, pl.ds(0, units)], sems.at[0]),
        pltpu.make_async_copy(up_ref, out_ref.at[:, pl.ds(units, units)], sems.at[1]),
    ]
    for j in range(units // rows):
        copies.append(
            pltpu.make_async_copy(
                down_ref.at[pl.ds(j * rows, rows)],
                out_ref.at[:, pl.ds(2 * units + j * rows, rows)],
                sems.at[2 + j],
            )
        )
    for copy in copies:
        copy.start()
    for copy in copies:
        copy.wait()


def host_place(z, core, depth, halves):
    return (z + depth // 2 + core * depth) % (depth * halves)


def natural_block(place, cores, ring):
    return (place % cores) * ring + place // cores


def dispatch_kernel(halves, depth, cores, ring, owners, x_ref, gain_ref, ids_ref, gates_ref, out_ref, mix_a_ref, mix_b_ref):
    tokens, width = x_ref.shape
    slots = owners * LOW
    half = width // 2
    x = x_ref[...].astype(F32)
    normed = (x * lax.rsqrt(jnp.mean(x * x, axis=-1, keepdims=True) + 1e-06) * gain_ref[...]).astype(BF16)
    step = width // (cores * ring)
    pieces = []
    for place in range(cores * ring):
        start = natural_block(place, cores, ring) * step
        pieces.append(normed[:, start : start + step])
    normed = jnp.concatenate(pieces, axis=1)

    lane = lax.broadcasted_iota(jnp.int32, (tokens, slots), 1)
    chip = lane // LOW
    across = owners // (halves * depth)
    turn = (chip // across + halves * depth - depth // 2) % (halves * depth)
    expert = (turn % depth * across + chip % across) * cores + turn // depth
    place = lane % LOW
    ids = ids_ref[...].T
    gates = gates_ref[...].T
    hot = jnp.zeros((tokens, slots), F32)
    gate = jnp.zeros((tokens, slots), F32)
    for k in range(ids.shape[1]):
        hit = ids[:, k : k + 1] == expert
        hot = jnp.where(hit, 1.0, hot)
        gate = jnp.where(hit, gates[:, k : k + 1], gate)
    row = lax.broadcasted_iota(jnp.int32, (tokens, tokens), 0)
    col = lax.broadcasted_iota(jnp.int32, (tokens, tokens), 1)
    earlier = jnp.where(col < row, 1.0, 0.0).astype(BF16)
    rank = jnp.dot(earlier, hot.astype(BF16), preferred_element_type=F32)
    rank = jnp.where(hot > 0.5, rank, -1.0)
    in_a = rank == place.astype(F32)
    in_b = rank == (LOW + place % FOLD).astype(F32)
    in_lo = in_b & (place < FOLD)
    in_hi = in_b & (place >= FOLD)

    def put(chosen):
        return jnp.where(chosen, 1.0, 0.0).astype(BF16)

    contract = (((0,), (0,)), ((), ()))
    out_ref[:, :width] = lax.dot_general(put(in_a), normed, contract, preferred_element_type=F32).astype(BF16)
    pick = jnp.concatenate([put(in_lo), put(in_hi)], axis=0)
    stacked = jnp.concatenate([normed[:, :half], normed[:, half:]], axis=0)
    out_ref[:, width:] = lax.dot_general(pick, stacked, contract, preferred_element_type=F32).astype(BF16)

    top = gate.astype(BF16).astype(F32)
    rest = gate - top

    def mix(chosen):
        return jnp.concatenate(
            [jnp.where(chosen, top, 0.0).astype(BF16), jnp.where(chosen, rest, 0.0).astype(BF16)], axis=0
        )

    mix_a_ref[...] = mix(in_a)
    mix_b_ref[:, :slots] = mix(in_lo)
    mix_b_ref[:, slots:] = mix(in_hi)


def expert_kernel(hidden_units, x_ref, w_hbm, out_ref, w_ref, sems):
    rows, cols = x_ref.shape
    width = w_ref.shape[0] * w_ref.shape[1]
    half = width // 2
    both = 2 * hidden_units
    block = w_ref.shape[1]
    count = w_ref.shape[0]

    chunks = sems.shape[0]
    per = count // chunks
    copies = []
    for i in range(chunks):
        at = pl.ds(i * per, per)
        copies.append(pltpu.make_async_copy(w_hbm.at[at], w_ref.at[at], sems.at[i]))
        copies[-1].start()
    sums_a, folds = None, [None, None]
    for i in range(chunks):
        copies[i].wait()
        piece = w_ref[i * per : (i + 1) * per, :, :both].reshape(per * block, both)
        start, side = i * per * block, 2 * i // chunks
        more = jnp.dot(x_ref[:, start : start + per * block], piece, preferred_element_type=F32)
        sums_a = more if sums_a is None else sums_a + more
        start = width + start - side * half
        more = jnp.dot(x_ref[:, start : start + per * block], piece, preferred_element_type=F32)
        folds[side] = more if folds[side] is None else folds[side] + more
    first = lax.broadcasted_iota(jnp.int32, (rows, both), 0) % LOW < FOLD
    sums_b = jnp.where(first, folds[0], folds[1])
    groups = sums_b.reshape(rows // LOW, LOW, both)
    sums_b = (groups + pltpu.roll(groups, FOLD, 1)).reshape(rows, both)

    def activate(sums):
        gate = sums[:, :hidden_units]
        return (gate / (1.0 + jnp.exp(-gate)) * sums[:, hidden_units:]).astype(BF16)

    hidden_a = activate(sums_a)
    hidden_b = activate(sums_b)

    def down(place):
        pieces = [w_ref[place, :, both + j * block : both + (j + 1) * block] for j in range(hidden_units // block)]
        return jnp.concatenate(pieces, axis=0)

    first_out = lax.broadcasted_iota(jnp.int32, (rows, 2 * block), 0) % LOW < FOLD
    for pair in range(count // 4):
        lo, hi = 2 * pair, count // 2 + 2 * pair
        low_d = jnp.concatenate([down(lo), down(lo + 1)], axis=1)
        high_d = jnp.concatenate([down(hi), down(hi + 1)], axis=1)
        out_ref[:, lo * block : (lo + 2) * block] = jnp.dot(
            hidden_a, low_d, preferred_element_type=F32
        ).astype(BF16)
        out_ref[:, hi * block : (hi + 2) * block] = jnp.dot(
            hidden_a, high_d, preferred_element_type=F32
        ).astype(BF16)
        out_ref[:, width + lo * block : width + (lo + 2) * block] = jnp.where(
            first_out,
            jnp.dot(hidden_b, low_d, preferred_element_type=F32),
            jnp.dot(hidden_b, high_d, preferred_element_type=F32),
        ).astype(BF16)


def combine_kernel(cores, ring, back_ref, mix_a_ref, mix_b_ref, out_ref):
    tokens, width = out_ref.shape
    half = width // 2
    slots = back_ref.shape[0]
    step = width // (cores * ring)
    folded = back_ref[:, width:]
    for side in range(2):
        both = jnp.dot(
            mix_a_ref[...], back_ref[:, side * half : (side + 1) * half], preferred_element_type=F32
        ) + jnp.dot(
            mix_b_ref[:, side * slots : (side + 1) * slots], folded, preferred_element_type=F32
        )
        total = (both[:tokens] + both[tokens:]).astype(BF16)
        for i in range(half // step):
            start = natural_block(side * (half // step) + i, cores, ring) * step
            out_ref[:, start : start + step] = total[:, i * step : (i + 1) * step]


def attend_kernel(halves, ring, heads_kv, q_ref, kv_hbm, place_ref, out_ref, kv_ref, sems):
    tokens, wide = q_ref.shape
    group = wide // HD // heads_kv
    blocks = halves * ring
    keys = blocks * tokens
    factor = math.log2(math.e) / math.sqrt(HD)
    kind = heads_kv * HD
    copies = []
    for i in range(2):
        at = (slice(None), slice(None), pl.ds(i * kind, kind))
        copies.append(pltpu.make_async_copy(kv_hbm.at[at], kv_ref.at[at], sems.at[i]))
        copies[i].start()
    lane = lax.broadcasted_iota(jnp.int32, (tokens, keys), 1)
    row = lax.broadcasted_iota(jnp.int32, (tokens, keys), 0)
    block = lane // tokens
    here = place_ref[0] // ring
    passed = jnp.where(here == 0, halves, 0)
    side = jnp.where(block % halves == 0, here, passed)
    key_pos = (side * ring + block // halves) * tokens + lane % tokens
    bias = jnp.where(key_pos <= row + place_ref[0] * tokens, 0.0, MASKED)
    ones = jnp.ones((keys, HD), BF16)
    copies[0].wait()
    for g in range(heads_kv):
        key = kv_ref[:, :, g * HD : (g + 1) * HD].reshape(keys, HD)
        for i in range(g * group, (g + 1) * group):
            at = slice(i * HD, (i + 1) * HD)
            scores = lax.dot_general(
                q_ref[:, at], key, (((1,), (1,)), ((), ())), preferred_element_type=F32
            )
            scores = scores * factor + bias
            probs = jnp.exp2(scores - jnp.max(scores, axis=-1, keepdims=True))
            if i == 0:
                copies[1].wait()
            if i == g * group:
                value = kv_ref[:, :, kind + g * HD : kind + (g + 1) * HD].reshape(keys, HD)
                value = jnp.concatenate([value, ones], axis=1)
            mixed = jnp.dot(probs.astype(BF16), value, preferred_element_type=F32)
            out_ref[:, at] = (mixed[:, :HD] / mixed[:, HD:]).astype(BF16)


def estimate(flops, bytes_accessed, transcendentals=0):
    return pl.CostEstimate(flops=flops, bytes_accessed=bytes_accessed, transcendentals=transcendentals)


def shards(
    queries, key_rows, value_rows, stream, norm_gain, expert_ids, gate_values, w_gate, w_up, w_down
):
    tokens, width = stream.shape[1:]
    heads_kv = key_rows.shape[2] // HD
    hidden_units = w_gate.shape[2]
    halves, ring, cores = lax.axis_size("zh"), lax.axis_size("y"), lax.axis_size("c")
    depth = lax.axis_size("zl")
    owners = lax.axis_size(DP)
    slots = owners * LOW
    wide = width + width // 2
    params = pltpu.CompilerParams(vmem_limit_bytes=48 * 1024 * 1024)

    with jax.named_scope("weights"):
        packed = pl.pallas_call(
            pack_kernel,
            out_shape=jax.ShapeDtypeStruct((w_gate.shape[1], 3 * hidden_units), BF16),
            in_specs=[HBM] * 3,
            out_specs=HBM,
            scratch_shapes=[pltpu.SemaphoreType.DMA((2 + hidden_units // tokens,))],
            name="pack",
        )(w_gate[0], w_up[0], w_down[0])
        route = []
        for h in range(halves):
            for z in range(depth):
                for c in range(cores):
                    to = host_place(z, c, depth, halves)
                    route.append(((h * depth + z) * cores + c, to * cores + h))
        part = lax.ppermute(packed, ("zh", "zl", "c"), route)
    with jax.named_scope("dispatch"):
        ids, _ = lax.optimization_barrier((expert_ids[0].T, packed))
        outgoing, mix_a, mix_b = pl.pallas_call(
            functools.partial(dispatch_kernel, halves, depth, cores, ring, owners),
            out_shape=(
                jax.ShapeDtypeStruct((slots, wide), BF16),
                jax.ShapeDtypeStruct((2 * tokens, slots), BF16),
                jax.ShapeDtypeStruct((2 * tokens, 2 * slots), BF16),
            ),
            in_specs=[VMEM] * 4,
            out_specs=(VMEM,) * 3,
            compiler_params=pltpu.CompilerParams(vmem_limit_bytes=65200 * 1024),
            cost_estimate=estimate(4 * 256 * 256 * 2048, 4 * 1024 * 1024),
            name="dispatch",
        )(stream[0], norm_gain[None, :], ids, gate_values[0].T)
        part, _ = lax.optimization_barrier((part, outgoing))
        weights = lax.all_gather(part, ("y", "c"), axis=0)
        arrived = lax.all_to_all(
            outgoing.reshape(owners, LOW, wide), CHIPS, split_axis=0, concat_axis=0, tiled=True
        ).reshape(slots, wide)

    with jax.named_scope("keys"):
        key_local, value_local, outgoing, part = lax.optimization_barrier(
            (key_rows[0], value_rows[0], outgoing, part)
        )
        kv = jnp.concatenate([key_local, value_local], axis=1)
        kv_passed = lax.ppermute(kv, "zh", [(0, 1)])
        kv_pair = jnp.stack([kv, kv_passed])
        kv_all = lax.all_gather(kv_pair, "y", axis=0, tiled=True)
        arrived, kv_pair = lax.optimization_barrier((arrived, kv_pair))

    with jax.named_scope("experts"):
        answers = pl.pallas_call(
            functools.partial(expert_kernel, hidden_units),
            out_shape=jax.ShapeDtypeStruct((slots, wide), BF16),
            in_specs=[VMEM, HBM],
            out_specs=VMEM,
            scratch_shapes=[pltpu.VMEM(weights.shape, BF16), pltpu.SemaphoreType.DMA((4,))],
            compiler_params=params,
            cost_estimate=estimate(6 * 512 * 2048 * 384, 8 * 1024 * 1024),
            name="experts",
        )(arrived, weights)
        returned = lax.all_to_all(
            answers.reshape(owners, LOW, wide), CHIPS, split_axis=0, concat_axis=0, tiled=True
        ).reshape(slots, wide)

    with jax.named_scope("attend"):
        place = lax.axis_index(CTX).astype(jnp.int32)[None]
        attended = pl.pallas_call(
            functools.partial(attend_kernel, halves, ring, heads_kv),
            out_shape=jax.ShapeDtypeStruct(queries.shape[1:], BF16),
            in_specs=[VMEM, HBM, SMEM],
            out_specs=VMEM,
            scratch_shapes=[
                pltpu.VMEM((halves * ring, tokens, 2 * heads_kv * HD), BF16),
                pltpu.SemaphoreType.DMA((2,)),
            ],
            compiler_params=pltpu.CompilerParams(vmem_limit_bytes=60 * 1024 * 1024),
            cost_estimate=estimate(4 * 2048 * 128 * 2048, 4 * 1024 * 1024, 16 * 128 * 2048),
            name="attend",
        )(queries[0], kv_all, place)

    with jax.named_scope("combine"):
        expert_out = pl.pallas_call(
            functools.partial(combine_kernel, cores, ring),
            out_shape=jax.ShapeDtypeStruct((tokens, width), BF16),
            in_specs=[VMEM] * 3,
            out_specs=VMEM,
            compiler_params=params,
            cost_estimate=estimate(2 * 256 * 512 * 2048, 3 * 1024 * 1024),
            name="combine",
        )(returned, mix_a, mix_b)
    return (attended[None], expert_out[None])


def solution(mesh):
    fine = Mesh(mesh.devices.reshape(2, 8, 4, 4, 2), CTX + DP)
    rows = P(DP, CTX, None)
    return jax.shard_map(
        shards,
        mesh=fine,
        in_specs=(rows, rows, rows, rows, P(), rows, rows, rows, rows, P(DP, None, CTX)),
        out_specs=(rows, rows),
        check_vma=False,
    )
```

```python
import functools
import math

import jax
import jax.numpy as jnp
from jax import lax
from jax.experimental import pallas as pl
from jax.experimental.pallas import tpu as pltpu
from jax.sharding import Mesh, PartitionSpec as P

HD = 128
CAP = 12
LOW = 8
FOLD = CAP - LOW
CTX = ("zh", "y")
DP = ("zl", "x", "c")
CHIPS = ("zh", "zl", "x")
MASKED = -1e30
F32 = jnp.float32
BF16 = jnp.bfloat16
VMEM = pl.BlockSpec(memory_space=pltpu.VMEM)
HBM = pl.BlockSpec(memory_space=pltpu.HBM)
SMEM = pl.BlockSpec(memory_space=pltpu.SMEM)


def pack_kernel(gate_ref, up_ref, down_ref, out_ref, sems):
    rows, units = gate_ref.shape
    copies = [
        pltpu.make_async_copy(gate_ref, out_ref.at[:, pl.ds(0, units)], sems.at[0]),
        pltpu.make_async_copy(up_ref, out_ref.at[:, pl.ds(units, units)], sems.at[1]),
    ]
    for j in range(units // rows):
        copies.append(
            pltpu.make_async_copy(
                down_ref.at[pl.ds(j * rows, rows)],
                out_ref.at[:, pl.ds(2 * units + j * rows, rows)],
                sems.at[2 + j],
            )
        )
    for copy in copies:
        copy.start()
    for copy in copies:
        copy.wait()


def host_place(z, core, depth, halves):
    return (z + depth // 2 + core * depth) % (depth * halves)


def natural_block(place, cores, ring):
    return (place % cores) * ring + place // cores


def dispatch_kernel(halves, depth, cores, ring, owners, x_ref, gain_ref, ids_ref, gates_ref, out_ref, mix_a_ref, mix_b_ref):
    tokens, width = x_ref.shape
    slots = owners * LOW
    half = width // 2
    x = x_ref[...].astype(F32)
    normed = (x * lax.rsqrt(jnp.mean(x * x, axis=-1, keepdims=True) + 1e-06) * gain_ref[...]).astype(BF16)
    step = width // (cores * ring)
    pieces = []
    for place in range(cores * ring):
        start = natural_block(place, cores, ring) * step
        pieces.append(normed[:, start : start + step])
    normed = jnp.concatenate(pieces, axis=1)

    lane = lax.broadcasted_iota(jnp.int32, (tokens, slots), 1)
    chip = lane // LOW
    across = owners // (halves * depth)
    turn = (chip // across + halves * depth - depth // 2) % (halves * depth)
    expert = (turn % depth * across + chip % across) * cores + turn // depth
    place = lane % LOW
    ids = ids_ref[...].T
    gates = gates_ref[...].T
    hot = jnp.zeros((tokens, slots), F32)
    gate = jnp.zeros((tokens, slots), F32)
    for k in range(ids.shape[1]):
        hit = ids[:, k : k + 1] == expert
        hot = jnp.where(hit, 1.0, hot)
        gate = jnp.where(hit, gates[:, k : k + 1], gate)
    row = lax.broadcasted_iota(jnp.int32, (tokens, tokens), 0)
    col = lax.broadcasted_iota(jnp.int32, (tokens, tokens), 1)
    earlier = jnp.where(col < row, 1.0, 0.0).astype(BF16)
    rank = jnp.dot(earlier, hot.astype(BF16), preferred_element_type=F32)
    rank = jnp.where(hot > 0.5, rank, -1.0)
    in_a = rank == place.astype(F32)
    in_b = rank == (LOW + place % FOLD).astype(F32)
    in_lo = in_b & (place < FOLD)
    in_hi = in_b & (place >= FOLD)

    def put(chosen):
        return jnp.where(chosen, 1.0, 0.0).astype(BF16)

    contract = (((0,), (0,)), ((), ()))
    out_ref[:, :width] = lax.dot_general(put(in_a), normed, contract, preferred_element_type=F32).astype(BF16)
    pick = jnp.concatenate([put(in_lo), put(in_hi)], axis=0)
    stacked = jnp.concatenate([normed[:, :half], normed[:, half:]], axis=0)
    out_ref[:, width:] = lax.dot_general(pick, stacked, contract, preferred_element_type=F32).astype(BF16)

    top = gate.astype(BF16).astype(F32)
    rest = gate - top

    def mix(chosen):
        return jnp.concatenate(
            [jnp.where(chosen, top, 0.0).astype(BF16), jnp.where(chosen, rest, 0.0).astype(BF16)], axis=0
        )

    mix_a_ref[...] = mix(in_a)
    mix_b_ref[:, :slots] = mix(in_lo)
    mix_b_ref[:, slots:] = mix(in_hi)


def expert_kernel(hidden_units, x_ref, w_hbm, out_ref, w_ref, sems):
    rows, cols = x_ref.shape
    width = w_ref.shape[0] * w_ref.shape[1]
    half = width // 2
    both = 2 * hidden_units
    block = w_ref.shape[1]
    count = w_ref.shape[0]

    chunks = sems.shape[0]
    per = count // chunks
    copies = []
    for i in range(chunks):
        at = pl.ds(i * per, per)
        copies.append(pltpu.make_async_copy(w_hbm.at[at], w_ref.at[at], sems.at[i]))
        copies[-1].start()
    sums_a, folds = None, [None, None]
    for i in range(chunks):
        copies[i].wait()
        piece = w_ref[i * per : (i + 1) * per, :, :both].reshape(per * block, both)
        start, side = i * per * block, 2 * i // chunks
        more = jnp.dot(x_ref[:, start : start + per * block], piece, preferred_element_type=F32)
        sums_a = more if sums_a is None else sums_a + more
        start = width + start - side * half
        more = jnp.dot(x_ref[:, start : start + per * block], piece, preferred_element_type=F32)
        folds[side] = more if folds[side] is None else folds[side] + more
    first = lax.broadcasted_iota(jnp.int32, (rows, both), 0) % LOW < FOLD
    sums_b = jnp.where(first, folds[0], folds[1])
    groups = sums_b.reshape(rows // LOW, LOW, both)
    sums_b = (groups + pltpu.roll(groups, FOLD, 1)).reshape(rows, both)

    def activate(sums):
        gate = sums[:, :hidden_units]
        return (gate / (1.0 + jnp.exp(-gate)) * sums[:, hidden_units:]).astype(BF16)

    hidden_a = activate(sums_a)
    hidden_b = activate(sums_b)

    def down(place):
        pieces = [w_ref[place, :, both + j * block : both + (j + 1) * block] for j in range(hidden_units // block)]
        return jnp.concatenate(pieces, axis=0)

    first_out = lax.broadcasted_iota(jnp.int32, (rows, 2 * block), 0) % LOW < FOLD
    for pair in range(count // 4):
        lo, hi = 2 * pair, count // 2 + 2 * pair
        low_d = jnp.concatenate([down(lo), down(lo + 1)], axis=1)
        high_d = jnp.concatenate([down(hi), down(hi + 1)], axis=1)
        out_ref[:, lo * block : (lo + 2) * block] = jnp.dot(
            hidden_a, low_d, preferred_element_type=F32
        ).astype(BF16)
        out_ref[:, hi * block : (hi + 2) * block] = jnp.dot(
            hidden_a, high_d, preferred_element_type=F32
        ).astype(BF16)
        out_ref[:, width + lo * block : width + (lo + 2) * block] = jnp.where(
            first_out,
            jnp.dot(hidden_b, low_d, preferred_element_type=F32),
            jnp.dot(hidden_b, high_d, preferred_element_type=F32),
        ).astype(BF16)


def combine_kernel(cores, ring, back_ref, mix_a_ref, mix_b_ref, out_ref):
    tokens, width = out_ref.shape
    half = width // 2
    slots = back_ref.shape[0]
    step = width // (cores * ring)
    folded = back_ref[:, width:]
    for side in range(2):
        both = jnp.dot(
            mix_a_ref[...], back_ref[:, side * half : (side + 1) * half], preferred_element_type=F32
        ) + jnp.dot(
            mix_b_ref[:, side * slots : (side + 1) * slots], folded, preferred_element_type=F32
        )
        total = (both[:tokens] + both[tokens:]).astype(BF16)
        for i in range(half // step):
            start = natural_block(side * (half // step) + i, cores, ring) * step
            out_ref[:, start : start + step] = total[:, i * step : (i + 1) * step]


def attend_kernel(halves, ring, heads_kv, q_ref, kv_hbm, place_ref, out_ref, kv_ref, sems):
    tokens, wide = q_ref.shape
    group = wide // HD // heads_kv
    keys = ring * tokens
    kind = heads_kv * HD
    factor = math.log2(math.e) / math.sqrt(HD)
    copies = []
    for side in range(halves):
        copies.append(pltpu.make_async_copy(kv_hbm.at[:, side], kv_ref.at[side], sems.at[side]))
        copies[side].start()
    here = place_ref[0] // ring
    mine = place_ref[0] % ring
    lane = lax.broadcasted_iota(jnp.int32, (tokens, keys), 1)
    row = lax.broadcasted_iota(jnp.int32, (tokens, keys), 0)
    bias = jnp.where(lane <= row + mine * tokens, 0.0, MASKED)
    for copy in copies:
        copy.wait()

    def attend(sides):
        ones = jnp.ones((sides * keys, HD), BF16)
        for g in range(heads_kv):
            key = kv_ref[:sides, :, :, g * HD : (g + 1) * HD].reshape(sides * keys, HD)
            value = kv_ref[:sides, :, :, kind + g * HD : kind + (g + 1) * HD].reshape(sides * keys, HD)
            value = jnp.concatenate([value, ones], axis=1)
            for i in range(g * group, (g + 1) * group):
                at = slice(i * HD, (i + 1) * HD)
                scores = lax.dot_general(
                    q_ref[:, at], key, (((1,), (1,)), ((), ())), preferred_element_type=F32
                )
                scores = scores * factor
                masked = scores[:, :keys] + bias
                scores = masked if sides == 1 else jnp.concatenate([masked, scores[:, keys:]], axis=1)
                probs = jnp.exp2(scores - jnp.max(scores, axis=-1, keepdims=True))
                mixed = jnp.dot(probs.astype(BF16), value, preferred_element_type=F32)
                out_ref[:, at] = (mixed[:, :HD] / mixed[:, HD:]).astype(BF16)

    @pl.when(here == 0)
    def _():
        attend(1)

    @pl.when(here > 0)
    def _():
        attend(halves)


def estimate(flops, bytes_accessed, transcendentals=0):
    return pl.CostEstimate(flops=flops, bytes_accessed=bytes_accessed, transcendentals=transcendentals)


def shards(
    queries, key_rows, value_rows, stream, norm_gain, expert_ids, gate_values, w_gate, w_up, w_down
):
    tokens, width = stream.shape[1:]
    heads_kv = key_rows.shape[2] // HD
    hidden_units = w_gate.shape[2]
    halves, ring, cores = lax.axis_size("zh"), lax.axis_size("y"), lax.axis_size("c")
    depth = lax.axis_size("zl")
    owners = lax.axis_size(DP)
    slots = owners * LOW
    wide = width + width // 2
    params = pltpu.CompilerParams(vmem_limit_bytes=48 * 1024 * 1024)

    with jax.named_scope("weights"):
        packed = pl.pallas_call(
            pack_kernel,
            out_shape=jax.ShapeDtypeStruct((w_gate.shape[1], 3 * hidden_units), BF16),
            in_specs=[HBM] * 3,
            out_specs=VMEM,
            scratch_shapes=[pltpu.SemaphoreType.DMA((2 + hidden_units // tokens,))],
            name="pack",
        )(w_gate[0], w_up[0], w_down[0])
        route = []
        for h in range(halves):
            for z in range(depth):
                for c in range(cores):
                    to = host_place(z, c, depth, halves)
                    route.append(((h * depth + z) * cores + c, to * cores + h))
        part = lax.ppermute(packed, ("zh", "zl", "c"), route)
    with jax.named_scope("dispatch"):
        ids, _ = lax.optimization_barrier((expert_ids[0].T, packed))
        outgoing, mix_a, mix_b = pl.pallas_call(
            functools.partial(dispatch_kernel, halves, depth, cores, ring, owners),
            out_shape=(
                jax.ShapeDtypeStruct((slots, wide), BF16),
                jax.ShapeDtypeStruct((2 * tokens, slots), BF16),
                jax.ShapeDtypeStruct((2 * tokens, 2 * slots), BF16),
            ),
            in_specs=[VMEM] * 4,
            out_specs=(VMEM,) * 3,
            compiler_params=pltpu.CompilerParams(vmem_limit_bytes=65200 * 1024),
            cost_estimate=estimate(4 * 256 * 256 * 2048, 4 * 1024 * 1024),
            name="dispatch",
        )(stream[0], norm_gain[None, :], ids, gate_values[0].T)
        arrived = lax.all_to_all(
            outgoing.reshape(owners, LOW, wide), CHIPS, split_axis=0, concat_axis=0, tiled=True
        ).reshape(slots, wide)

    with jax.named_scope("keys"):
        key_local, value_local, _ = lax.optimization_barrier((key_rows[0], value_rows[0], outgoing))
        kv = jnp.concatenate([key_local, value_local], axis=1)
        part, kv = lax.optimization_barrier((part, kv))
        weights = lax.all_gather(part, ("y", "c"), axis=0)
        kv_passed = lax.ppermute(kv, "zh", [(0, 1)])
        kv_pair = jnp.stack([kv, kv_passed])
        kv_all = lax.all_gather(kv_pair, "y", axis=0)
        arrived, kv_pair = lax.optimization_barrier((arrived, kv_pair))

    with jax.named_scope("experts"):
        answers = pl.pallas_call(
            functools.partial(expert_kernel, hidden_units),
            out_shape=jax.ShapeDtypeStruct((slots, wide), BF16),
            in_specs=[VMEM, HBM],
            out_specs=VMEM,
            scratch_shapes=[pltpu.VMEM(weights.shape, BF16), pltpu.SemaphoreType.DMA((4,))],
            compiler_params=params,
            cost_estimate=estimate(6 * 512 * 2048 * 384, 8 * 1024 * 1024),
            name="experts",
        )(arrived, weights)
        returned = lax.all_to_all(
            answers.reshape(owners, LOW, wide), CHIPS, split_axis=0, concat_axis=0, tiled=True
        ).reshape(slots, wide)

    with jax.named_scope("attend"):
        place = lax.axis_index(CTX).astype(jnp.int32)[None]
        attended = pl.pallas_call(
            functools.partial(attend_kernel, halves, ring, heads_kv),
            out_shape=jax.ShapeDtypeStruct(queries.shape[1:], BF16),
            in_specs=[VMEM, HBM, SMEM],
            out_specs=VMEM,
            scratch_shapes=[
                pltpu.VMEM((halves, ring, tokens, 2 * heads_kv * HD), BF16),
                pltpu.SemaphoreType.DMA((2,)),
            ],
            compiler_params=pltpu.CompilerParams(vmem_limit_bytes=60 * 1024 * 1024),
            cost_estimate=estimate(4 * 2048 * 128 * 2048, 4 * 1024 * 1024, 16 * 128 * 2048),
            name="attend",
        )(queries[0], kv_all, place)

    with jax.named_scope("combine"):
        expert_out = pl.pallas_call(
            functools.partial(combine_kernel, cores, ring),
            out_shape=jax.ShapeDtypeStruct((tokens, width), BF16),
            in_specs=[VMEM] * 3,
            out_specs=VMEM,
            compiler_params=params,
            cost_estimate=estimate(2 * 256 * 512 * 2048, 3 * 1024 * 1024),
            name="combine",
        )(returned, mix_a, mix_b)
    return (attended[None], expert_out[None])


def solution(mesh):
    fine = Mesh(mesh.devices.reshape(2, 8, 4, 4, 2), CTX + DP)
    rows = P(DP, CTX, None)
    return jax.shard_map(
        shards,
        mesh=fine,
        in_specs=(rows, rows, rows, rows, P(), rows, rows, rows, rows, P(DP, None, CTX)),
        out_specs=(rows, rows),
        check_vma=False,
    )
```

```python
import functools
import math

import jax
import jax.numpy as jnp
from jax import lax
from jax.experimental import pallas as pl
from jax.experimental.pallas import tpu as pltpu
from jax.sharding import Mesh, PartitionSpec as P

HD = 128
CAP = 12
LOW = 8
FOLD = CAP - LOW
CTX = ("zh", "y")
DP = ("zl", "x", "c")
CHIPS = ("zh", "zl", "x")
MASKED = -1e30
F32 = jnp.float32
BF16 = jnp.bfloat16
VMEM = pl.BlockSpec(memory_space=pltpu.VMEM)
HBM = pl.BlockSpec(memory_space=pltpu.HBM)
SMEM = pl.BlockSpec(memory_space=pltpu.SMEM)


def pack_kernel(gate_ref, up_ref, down_ref, out_ref, sems):
    rows, units = gate_ref.shape
    copies = [
        pltpu.make_async_copy(gate_ref, out_ref.at[:, pl.ds(0, units)], sems.at[0]),
        pltpu.make_async_copy(up_ref, out_ref.at[:, pl.ds(units, units)], sems.at[1]),
    ]
    for j in range(units // rows):
        copies.append(
            pltpu.make_async_copy(
                down_ref.at[pl.ds(j * rows, rows)],
                out_ref.at[:, pl.ds(2 * units + j * rows, rows)],
                sems.at[2 + j],
            )
        )
    for copy in copies:
        copy.start()
    for copy in copies:
        copy.wait()


def host_place(z, core, depth, halves):
    return (z + depth // 2 + core * depth) % (depth * halves)


def natural_block(place, cores, ring):
    return (place % cores) * ring + place // cores


def dispatch_kernel(halves, depth, cores, ring, owners, x_ref, gain_ref, ids_ref, gates_ref, out_ref, mix_a_ref, mix_b_ref):
    tokens, width = x_ref.shape
    slots = owners * LOW
    half = width // 2
    x = x_ref[...].astype(F32)
    normed = (x * lax.rsqrt(jnp.mean(x * x, axis=-1, keepdims=True) + 1e-06) * gain_ref[...]).astype(BF16)
    step = width // (cores * ring)
    pieces = []
    for place in range(cores * ring):
        start = natural_block(place, cores, ring) * step
        pieces.append(normed[:, start : start + step])
    normed = jnp.concatenate(pieces, axis=1)

    lane = lax.broadcasted_iota(jnp.int32, (tokens, slots), 1)
    chip = lane // LOW
    across = owners // (halves * depth)
    turn = (chip // across + halves * depth - depth // 2) % (halves * depth)
    expert = (turn % depth * across + chip % across) * cores + turn // depth
    place = lane % LOW
    ids = ids_ref[...].T
    gates = gates_ref[...].T
    hot = jnp.zeros((tokens, slots), F32)
    gate = jnp.zeros((tokens, slots), F32)
    for k in range(ids.shape[1]):
        hit = ids[:, k : k + 1] == expert
        hot = jnp.where(hit, 1.0, hot)
        gate = jnp.where(hit, gates[:, k : k + 1], gate)
    row = lax.broadcasted_iota(jnp.int32, (tokens, tokens), 0)
    col = lax.broadcasted_iota(jnp.int32, (tokens, tokens), 1)
    earlier = jnp.where(col < row, 1.0, 0.0).astype(BF16)
    rank = jnp.dot(earlier, hot.astype(BF16), preferred_element_type=F32)
    rank = jnp.where(hot > 0.5, rank, -1.0)
    in_a = rank == place.astype(F32)
    in_b = rank == (LOW + place % FOLD).astype(F32)
    in_lo = in_b & (place < FOLD)
    in_hi = in_b & (place >= FOLD)

    def put(chosen):
        return jnp.where(chosen, 1.0, 0.0).astype(BF16)

    contract = (((0,), (0,)), ((), ()))
    out_ref[:, :width] = lax.dot_general(put(in_a), normed, contract, preferred_element_type=F32).astype(BF16)
    pick = jnp.concatenate([put(in_lo), put(in_hi)], axis=0)
    stacked = jnp.concatenate([normed[:, :half], normed[:, half:]], axis=0)
    out_ref[:, width:] = lax.dot_general(pick, stacked, contract, preferred_element_type=F32).astype(BF16)

    top = gate.astype(BF16).astype(F32)
    rest = gate - top

    def mix(chosen):
        return jnp.concatenate(
            [jnp.where(chosen, top, 0.0).astype(BF16), jnp.where(chosen, rest, 0.0).astype(BF16)], axis=0
        )

    mix_a_ref[...] = mix(in_a)
    mix_b_ref[:, :slots] = mix(in_lo)
    mix_b_ref[:, slots:] = mix(in_hi)


def expert_kernel(hidden_units, x_ref, w_hbm, out_ref, w_ref, sems):
    rows, cols = x_ref.shape
    width = w_ref.shape[0] * w_ref.shape[1]
    half = width // 2
    both = 2 * hidden_units
    block = w_ref.shape[1]
    count = w_ref.shape[0]

    chunks = sems.shape[0]
    per = count // chunks
    copies = []
    for i in range(chunks):
        at = pl.ds(i * per, per)
        copies.append(pltpu.make_async_copy(w_hbm.at[at], w_ref.at[at], sems.at[i]))
        copies[-1].start()
    sums_a, folds = None, [None, None]
    for i in range(chunks):
        copies[i].wait()
        piece = w_ref[i * per : (i + 1) * per, :, :both].reshape(per * block, both)
        start, side = i * per * block, 2 * i // chunks
        more = jnp.dot(x_ref[:, start : start + per * block], piece, preferred_element_type=F32)
        sums_a = more if sums_a is None else sums_a + more
        start = width + start - side * half
        more = jnp.dot(x_ref[:, start : start + per * block], piece, preferred_element_type=F32)
        folds[side] = more if folds[side] is None else folds[side] + more
    first = lax.broadcasted_iota(jnp.int32, (rows, both), 0) % LOW < FOLD
    sums_b = jnp.where(first, folds[0], folds[1])
    groups = sums_b.reshape(rows // LOW, LOW, both)
    sums_b = (groups + pltpu.roll(groups, FOLD, 1)).reshape(rows, both)

    def activate(sums):
        gate = sums[:, :hidden_units]
        return (gate / (1.0 + jnp.exp(-gate)) * sums[:, hidden_units:]).astype(BF16)

    hidden_a = activate(sums_a)
    hidden_b = activate(sums_b)

    def down(place):
        pieces = [w_ref[place, :, both + j * block : both + (j + 1) * block] for j in range(hidden_units // block)]
        return jnp.concatenate(pieces, axis=0)

    first_out = lax.broadcasted_iota(jnp.int32, (rows, 2 * block), 0) % LOW < FOLD
    for pair in range(count // 4):
        lo, hi = 2 * pair, count // 2 + 2 * pair
        low_d = jnp.concatenate([down(lo), down(lo + 1)], axis=1)
        high_d = jnp.concatenate([down(hi), down(hi + 1)], axis=1)
        out_ref[:, lo * block : (lo + 2) * block] = jnp.dot(
            hidden_a, low_d, preferred_element_type=F32
        ).astype(BF16)
        out_ref[:, hi * block : (hi + 2) * block] = jnp.dot(
            hidden_a, high_d, preferred_element_type=F32
        ).astype(BF16)
        out_ref[:, width + lo * block : width + (lo + 2) * block] = jnp.where(
            first_out,
            jnp.dot(hidden_b, low_d, preferred_element_type=F32),
            jnp.dot(hidden_b, high_d, preferred_element_type=F32),
        ).astype(BF16)


def combine_kernel(cores, ring, back_ref, mix_a_ref, mix_b_ref, out_ref):
    tokens, width = out_ref.shape
    half = width // 2
    slots = back_ref.shape[0]
    step = width // (cores * ring)
    folded = back_ref[:, width:]
    for side in range(2):
        both = jnp.dot(
            mix_a_ref[...], back_ref[:, side * half : (side + 1) * half], preferred_element_type=F32
        ) + jnp.dot(
            mix_b_ref[:, side * slots : (side + 1) * slots], folded, preferred_element_type=F32
        )
        total = (both[:tokens] + both[tokens:]).astype(BF16)
        for i in range(half // step):
            start = natural_block(side * (half // step) + i, cores, ring) * step
            out_ref[:, start : start + step] = total[:, i * step : (i + 1) * step]


def attend_kernel(halves, ring, heads_kv, q_ref, kv_hbm, place_ref, out_ref, kv_ref, sems):
    tokens, wide = q_ref.shape
    group = wide // HD // heads_kv
    keys = ring * tokens
    kind = heads_kv * HD
    factor = math.log2(math.e) / math.sqrt(HD)
    copies = []
    for side in range(halves):
        copies.append(pltpu.make_async_copy(kv_hbm.at[:, side], kv_ref.at[side], sems.at[side]))
        copies[side].start()
    here = place_ref[0] // ring
    mine = place_ref[0] % ring
    lane = lax.broadcasted_iota(jnp.int32, (tokens, keys), 1)
    row = lax.broadcasted_iota(jnp.int32, (tokens, keys), 0)
    bias = jnp.where(lane <= row + mine * tokens, 0.0, MASKED)
    for copy in copies:
        copy.wait()

    def attend(sides):
        ones = jnp.ones((sides * keys, HD), BF16)
        for g in range(heads_kv):
            key = kv_ref[:sides, :, :, g * HD : (g + 1) * HD].reshape(sides * keys, HD)
            value = kv_ref[:sides, :, :, kind + g * HD : kind + (g + 1) * HD].reshape(sides * keys, HD)
            value = jnp.concatenate([value, ones], axis=1)
            for i in range(g * group, (g + 1) * group):
                at = slice(i * HD, (i + 1) * HD)
                scores = lax.dot_general(
                    q_ref[:, at], key, (((1,), (1,)), ((), ())), preferred_element_type=F32
                )
                scores = scores * factor
                masked = scores[:, :keys] + bias
                scores = masked if sides == 1 else jnp.concatenate([masked, scores[:, keys:]], axis=1)
                probs = jnp.exp2(scores - jnp.max(scores, axis=-1, keepdims=True))
                mixed = jnp.dot(probs.astype(BF16), value, preferred_element_type=F32)
                out_ref[:, at] = (mixed[:, :HD] / mixed[:, HD:]).astype(BF16)

    @pl.when(here == 0)
    def _():
        attend(1)

    @pl.when(here > 0)
    def _():
        attend(halves)


def estimate(flops, bytes_accessed, transcendentals=0):
    return pl.CostEstimate(flops=flops, bytes_accessed=bytes_accessed, transcendentals=transcendentals)


def shards(
    queries, key_rows, value_rows, stream, norm_gain, expert_ids, gate_values, w_gate, w_up, w_down
):
    tokens, width = stream.shape[1:]
    heads_kv = key_rows.shape[2] // HD
    hidden_units = w_gate.shape[2]
    halves, ring, cores = lax.axis_size("zh"), lax.axis_size("y"), lax.axis_size("c")
    depth = lax.axis_size("zl")
    owners = lax.axis_size(DP)
    slots = owners * LOW
    wide = width + width // 2
    params = pltpu.CompilerParams(vmem_limit_bytes=48 * 1024 * 1024)

    with jax.named_scope("weights"):
        packed = pl.pallas_call(
            pack_kernel,
            out_shape=jax.ShapeDtypeStruct((w_gate.shape[1], 3 * hidden_units), BF16),
            in_specs=[HBM] * 3,
            out_specs=VMEM,
            scratch_shapes=[pltpu.SemaphoreType.DMA((2 + hidden_units // tokens,))],
            name="pack",
        )(w_gate[0], w_up[0], w_down[0])
        route = []
        for h in range(halves):
            for z in range(depth):
                for c in range(cores):
                    to = host_place(z, c, depth, halves)
                    route.append(((h * depth + z) * cores + c, to * cores + h))
        part = lax.ppermute(packed, ("zh", "zl", "c"), route)
    with jax.named_scope("dispatch"):
        ids, _ = lax.optimization_barrier((expert_ids[0].T, packed))
        outgoing, mix_a, mix_b = pl.pallas_call(
            functools.partial(dispatch_kernel, halves, depth, cores, ring, owners),
            out_shape=(
                jax.ShapeDtypeStruct((slots, wide), BF16),
                jax.ShapeDtypeStruct((2 * tokens, slots), BF16),
                jax.ShapeDtypeStruct((2 * tokens, 2 * slots), BF16),
            ),
            in_specs=[VMEM] * 4,
            out_specs=(VMEM,) * 3,
            compiler_params=pltpu.CompilerParams(vmem_limit_bytes=65200 * 1024),
            cost_estimate=estimate(4 * 256 * 256 * 2048, 4 * 1024 * 1024),
            name="dispatch",
        )(stream[0], norm_gain[None, :], ids, gate_values[0].T)
        arrived = lax.all_to_all(
            outgoing.reshape(owners, LOW, wide), CHIPS, split_axis=0, concat_axis=0, tiled=True
        ).reshape(slots, wide)

    with jax.named_scope("keys"):
        key_local, value_local, _ = lax.optimization_barrier((key_rows[0], value_rows[0], outgoing))
        kv = jnp.concatenate([key_local, value_local], axis=1)
        part, kv = lax.optimization_barrier((part, kv))
        weights = lax.all_gather(part, ("y", "c"), axis=0)
        deep = halves * depth
        kv_passed = kv
        for leg in range(2):
            route = [((z - leg * depth // 2) % deep, (z - (leg + 1) * depth // 2) % deep) for z in range(depth)]
            kv_passed = lax.ppermute(kv_passed, ("zh", "zl"), route)
        kv_pair = jnp.stack([kv, kv_passed])
        kv_all = lax.all_gather(kv_pair, "y", axis=0)
        arrived, kv_pair = lax.optimization_barrier((arrived, kv_pair))

    with jax.named_scope("experts"):
        answers = pl.pallas_call(
            functools.partial(expert_kernel, hidden_units),
            out_shape=jax.ShapeDtypeStruct((slots, wide), BF16),
            in_specs=[VMEM, HBM],
            out_specs=VMEM,
            scratch_shapes=[pltpu.VMEM(weights.shape, BF16), pltpu.SemaphoreType.DMA((4,))],
            compiler_params=params,
            cost_estimate=estimate(6 * 512 * 2048 * 384, 8 * 1024 * 1024),
            name="experts",
        )(arrived, weights)
        returned = lax.all_to_all(
            answers.reshape(owners, LOW, wide), CHIPS, split_axis=0, concat_axis=0, tiled=True
        ).reshape(slots, wide)

    with jax.named_scope("attend"):
        place = lax.axis_index(CTX).astype(jnp.int32)[None]
        attended = pl.pallas_call(
            functools.partial(attend_kernel, halves, ring, heads_kv),
            out_shape=jax.ShapeDtypeStruct(queries.shape[1:], BF16),
            in_specs=[VMEM, HBM, SMEM],
            out_specs=VMEM,
            scratch_shapes=[
                pltpu.VMEM((halves, ring, tokens, 2 * heads_kv * HD), BF16),
                pltpu.SemaphoreType.DMA((2,)),
            ],
            compiler_params=pltpu.CompilerParams(vmem_limit_bytes=60 * 1024 * 1024),
            cost_estimate=estimate(4 * 2048 * 128 * 2048, 4 * 1024 * 1024, 16 * 128 * 2048),
            name="attend",
        )(queries[0], kv_all, place)

    with jax.named_scope("combine"):
        expert_out = pl.pallas_call(
            functools.partial(combine_kernel, cores, ring),
            out_shape=jax.ShapeDtypeStruct((tokens, width), BF16),
            in_specs=[VMEM] * 3,
            out_specs=VMEM,
            compiler_params=params,
            cost_estimate=estimate(2 * 256 * 512 * 2048, 3 * 1024 * 1024),
            name="combine",
        )(returned, mix_a, mix_b)
    return (attended[None], expert_out[None])


def solution(mesh):
    fine = Mesh(mesh.devices.reshape(2, 8, 4, 4, 2), CTX + DP)
    rows = P(DP, CTX, None)
    return jax.shard_map(
        shards,
        mesh=fine,
        in_specs=(rows, rows, rows, rows, P(), rows, rows, rows, rows, P(DP, None, CTX)),
        out_specs=(rows, rows),
        check_vma=False,
    )
```

```python
import functools
import math

import jax
import jax.numpy as jnp
from jax import lax
from jax.experimental import pallas as pl
from jax.experimental.pallas import tpu as pltpu
from jax.sharding import Mesh, PartitionSpec as P

HD = 128
CAP = 12
LOW = 8
FOLD = CAP - LOW
CTX = ("zh", "y")
DP = ("zl", "x", "c")
CHIPS = ("zh", "zl", "x")
MASKED = -1e30
F32 = jnp.float32
BF16 = jnp.bfloat16
VMEM = pl.BlockSpec(memory_space=pltpu.VMEM)
HBM = pl.BlockSpec(memory_space=pltpu.HBM)
SMEM = pl.BlockSpec(memory_space=pltpu.SMEM)


def pack_kernel(gate_ref, up_ref, down_ref, out_ref, sems):
    rows, units = gate_ref.shape
    copies = [
        pltpu.make_async_copy(gate_ref, out_ref.at[:, pl.ds(0, units)], sems.at[0]),
        pltpu.make_async_copy(up_ref, out_ref.at[:, pl.ds(units, units)], sems.at[1]),
    ]
    for j in range(units // rows):
        copies.append(
            pltpu.make_async_copy(
                down_ref.at[pl.ds(j * rows, rows)],
                out_ref.at[:, pl.ds(2 * units + j * rows, rows)],
                sems.at[2 + j],
            )
        )
    for copy in copies:
        copy.start()
    for copy in copies:
        copy.wait()


def host_place(z, core, depth, halves):
    return (z + depth // 2 + core * depth) % (depth * halves)


def natural_block(place, cores, ring):
    return (place % cores) * ring + place // cores


def dispatch_kernel(halves, depth, cores, ring, owners, x_ref, gain_ref, ids_ref, gates_ref, out_ref, mix_a_ref, mix_b_ref):
    tokens, width = x_ref.shape
    slots = owners * LOW
    half = width // 2
    x = x_ref[...].astype(F32)
    normed = (x * lax.rsqrt(jnp.mean(x * x, axis=-1, keepdims=True) + 1e-06) * gain_ref[...]).astype(BF16)
    step = width // (cores * ring)
    pieces = []
    for place in range(cores * ring):
        start = natural_block(place, cores, ring) * step
        pieces.append(normed[:, start : start + step])
    normed = jnp.concatenate(pieces, axis=1)

    lane = lax.broadcasted_iota(jnp.int32, (tokens, slots), 1)
    chip = lane // LOW
    across = owners // (halves * depth)
    turn = (chip // across + halves * depth - depth // 2) % (halves * depth)
    expert = (turn % depth * across + chip % across) * cores + turn // depth
    place = lane % LOW
    ids = ids_ref[...].T
    gates = gates_ref[...].T
    hot = jnp.zeros((tokens, slots), F32)
    gate = jnp.zeros((tokens, slots), F32)
    for k in range(ids.shape[1]):
        hit = ids[:, k : k + 1] == expert
        hot = jnp.where(hit, 1.0, hot)
        gate = jnp.where(hit, gates[:, k : k + 1], gate)
    row = lax.broadcasted_iota(jnp.int32, (tokens, tokens), 0)
    col = lax.broadcasted_iota(jnp.int32, (tokens, tokens), 1)
    earlier = jnp.where(col < row, 1.0, 0.0).astype(BF16)
    rank = jnp.dot(earlier, hot.astype(BF16), preferred_element_type=F32)
    rank = jnp.where(hot > 0.5, rank, -1.0)
    in_a = rank == place.astype(F32)
    in_b = rank == (LOW + place % FOLD).astype(F32)
    in_lo = in_b & (place < FOLD)
    in_hi = in_b & (place >= FOLD)

    def put(chosen):
        return jnp.where(chosen, 1.0, 0.0).astype(BF16)

    contract = (((0,), (0,)), ((), ()))
    out_ref[:, :width] = lax.dot_general(put(in_a), normed, contract, preferred_element_type=F32).astype(BF16)
    pick = jnp.concatenate([put(in_lo), put(in_hi)], axis=0)
    stacked = jnp.concatenate([normed[:, :half], normed[:, half:]], axis=0)
    out_ref[:, width:] = lax.dot_general(pick, stacked, contract, preferred_element_type=F32).astype(BF16)

    top = gate.astype(BF16).astype(F32)
    rest = gate - top

    def mix(chosen):
        return jnp.concatenate(
            [jnp.where(chosen, top, 0.0).astype(BF16), jnp.where(chosen, rest, 0.0).astype(BF16)], axis=0
        )

    mix_a_ref[...] = mix(in_a)
    mix_b_ref[:, :slots] = mix(in_lo)
    mix_b_ref[:, slots:] = mix(in_hi)


def expert_kernel(hidden_units, x_ref, w_hbm, out_ref, w_ref, sems):
    rows, cols = x_ref.shape
    width = w_ref.shape[0] * w_ref.shape[1]
    half = width // 2
    both = 2 * hidden_units
    block = w_ref.shape[1]
    count = w_ref.shape[0]

    chunks = sems.shape[0]
    per = count // chunks
    copies = []
    for i in range(chunks):
        at = pl.ds(i * per, per)
        copies.append(pltpu.make_async_copy(w_hbm.at[at], w_ref.at[at], sems.at[i]))
        copies[-1].start()
    sums_a, folds = None, [None, None]
    for i in range(chunks):
        copies[i].wait()
        piece = w_ref[i * per : (i + 1) * per, :, :both].reshape(per * block, both)
        start, side = i * per * block, 2 * i // chunks
        more = jnp.dot(x_ref[:, start : start + per * block], piece, preferred_element_type=F32)
        sums_a = more if sums_a is None else sums_a + more
        start = width + start - side * half
        more = jnp.dot(x_ref[:, start : start + per * block], piece, preferred_element_type=F32)
        folds[side] = more if folds[side] is None else folds[side] + more
    first = lax.broadcasted_iota(jnp.int32, (rows, both), 0) % LOW < FOLD
    sums_b = jnp.where(first, folds[0], folds[1])
    groups = sums_b.reshape(rows // LOW, LOW, both)
    sums_b = (groups + pltpu.roll(groups, FOLD, 1)).reshape(rows, both)

    def activate(sums):
        gate = sums[:, :hidden_units]
        return (gate / (1.0 + jnp.exp(-gate)) * sums[:, hidden_units:]).astype(BF16)

    hidden_a = activate(sums_a)
    hidden_b = activate(sums_b)

    def down(place):
        pieces = [w_ref[place, :, both + j * block : both + (j + 1) * block] for j in range(hidden_units // block)]
        return jnp.concatenate(pieces, axis=0)

    first_out = lax.broadcasted_iota(jnp.int32, (rows, 2 * block), 0) % LOW < FOLD
    for pair in range(count // 4):
        lo, hi = 2 * pair, count // 2 + 2 * pair
        low_d = jnp.concatenate([down(lo), down(lo + 1)], axis=1)
        high_d = jnp.concatenate([down(hi), down(hi + 1)], axis=1)
        out_ref[:, lo * block : (lo + 2) * block] = jnp.dot(
            hidden_a, low_d, preferred_element_type=F32
        ).astype(BF16)
        out_ref[:, hi * block : (hi + 2) * block] = jnp.dot(
            hidden_a, high_d, preferred_element_type=F32
        ).astype(BF16)
        out_ref[:, width + lo * block : width + (lo + 2) * block] = jnp.where(
            first_out,
            jnp.dot(hidden_b, low_d, preferred_element_type=F32),
            jnp.dot(hidden_b, high_d, preferred_element_type=F32),
        ).astype(BF16)


def combine_kernel(cores, ring, back_ref, mix_a_ref, mix_b_ref, out_ref):
    tokens, width = out_ref.shape
    half = width // 2
    slots = back_ref.shape[0]
    step = width // (cores * ring)
    folded = back_ref[:, width:]
    for side in range(2):
        both = jnp.dot(
            mix_a_ref[...], back_ref[:, side * half : (side + 1) * half], preferred_element_type=F32
        ) + jnp.dot(
            mix_b_ref[:, side * slots : (side + 1) * slots], folded, preferred_element_type=F32
        )
        total = (both[:tokens] + both[tokens:]).astype(BF16)
        for i in range(half // step):
            start = natural_block(side * (half // step) + i, cores, ring) * step
            out_ref[:, start : start + step] = total[:, i * step : (i + 1) * step]


def attend_kernel(halves, ring, heads_kv, q_ref, kv_hbm, place_ref, out_ref, kv_ref, sems):
    tokens, wide = q_ref.shape
    group = wide // HD // heads_kv
    keys = ring * tokens
    kind = heads_kv * HD
    factor = math.log2(math.e) / math.sqrt(HD)
    copies = []
    for side in range(halves):
        copies.append(pltpu.make_async_copy(kv_hbm.at[:, side], kv_ref.at[side], sems.at[side]))
        copies[side].start()
    here = place_ref[0] // ring
    mine = place_ref[0] % ring
    lane = lax.broadcasted_iota(jnp.int32, (tokens, keys), 1)
    row = lax.broadcasted_iota(jnp.int32, (tokens, keys), 0)
    bias = jnp.where(lane <= row + mine * tokens, 0.0, MASKED)
    for copy in copies:
        copy.wait()

    def attend(sides):
        ones = jnp.ones((sides * keys, HD), BF16)
        for g in range(heads_kv):
            key = kv_ref[:sides, :, :, g * HD : (g + 1) * HD].reshape(sides * keys, HD)
            value = kv_ref[:sides, :, :, kind + g * HD : kind + (g + 1) * HD].reshape(sides * keys, HD)
            value = jnp.concatenate([value, ones], axis=1)
            for i in range(g * group, (g + 1) * group):
                at = slice(i * HD, (i + 1) * HD)
                scores = lax.dot_general(
                    q_ref[:, at], key, (((1,), (1,)), ((), ())), preferred_element_type=F32
                )
                scores = scores * factor
                masked = scores[:, :keys] + bias
                scores = masked if sides == 1 else jnp.concatenate([masked, scores[:, keys:]], axis=1)
                probs = jnp.exp2(scores - jnp.max(scores, axis=-1, keepdims=True))
                mixed = jnp.dot(probs.astype(BF16), value, preferred_element_type=F32)
                out_ref[:, at] = (mixed[:, :HD] / mixed[:, HD:]).astype(BF16)

    @pl.when(here == 0)
    def _():
        attend(1)

    @pl.when(here > 0)
    def _():
        attend(halves)


def estimate(flops, bytes_accessed, transcendentals=0):
    return pl.CostEstimate(flops=flops, bytes_accessed=bytes_accessed, transcendentals=transcendentals)


def shards(
    queries, key_rows, value_rows, stream, norm_gain, expert_ids, gate_values, w_gate, w_up, w_down
):
    tokens, width = stream.shape[1:]
    heads_kv = key_rows.shape[2] // HD
    hidden_units = w_gate.shape[2]
    halves, ring, cores = lax.axis_size("zh"), lax.axis_size("y"), lax.axis_size("c")
    depth = lax.axis_size("zl")
    owners = lax.axis_size(DP)
    slots = owners * LOW
    wide = width + width // 2
    params = pltpu.CompilerParams(vmem_limit_bytes=48 * 1024 * 1024)

    with jax.named_scope("weights"):
        packed = pl.pallas_call(
            pack_kernel,
            out_shape=jax.ShapeDtypeStruct((w_gate.shape[1], 3 * hidden_units), BF16),
            in_specs=[HBM] * 3,
            out_specs=VMEM,
            scratch_shapes=[pltpu.SemaphoreType.DMA((2 + hidden_units // tokens,))],
            name="pack",
        )(w_gate[0], w_up[0], w_down[0])
        route = []
        for h in range(halves):
            for z in range(depth):
                for c in range(cores):
                    to = host_place(z, c, depth, halves)
                    route.append(((h * depth + z) * cores + c, to * cores + h))
        part = lax.ppermute(packed, ("zh", "zl", "c"), route)
    with jax.named_scope("dispatch"):
        ids, _ = lax.optimization_barrier((expert_ids[0].T, packed))
        outgoing, mix_a, mix_b = pl.pallas_call(
            functools.partial(dispatch_kernel, halves, depth, cores, ring, owners),
            out_shape=(
                jax.ShapeDtypeStruct((slots, wide), BF16),
                jax.ShapeDtypeStruct((2 * tokens, slots), BF16),
                jax.ShapeDtypeStruct((2 * tokens, 2 * slots), BF16),
            ),
            in_specs=[VMEM] * 4,
            out_specs=(VMEM,) * 3,
            compiler_params=pltpu.CompilerParams(vmem_limit_bytes=65200 * 1024),
            cost_estimate=estimate(4 * 256 * 256 * 2048, 4 * 1024 * 1024),
            name="dispatch",
        )(stream[0], norm_gain[None, :], ids, gate_values[0].T)
        arrived = lax.all_to_all(
            outgoing.reshape(owners, LOW, wide), CHIPS, split_axis=0, concat_axis=0, tiled=True
        ).reshape(slots, wide)

    with jax.named_scope("keys"):
        key_local, value_local, _ = lax.optimization_barrier((key_rows[0], value_rows[0], outgoing))
        kv = jnp.concatenate([key_local, value_local], axis=1)
        part, kv = lax.optimization_barrier((part, kv))
        weights = lax.all_gather(part, ("y", "c"), axis=0)
        deep = halves * depth
        kv_passed = kv
        for leg in range(2):
            route = [((z + leg * depth // 2) % deep, (z + (leg + 1) * depth // 2) % deep) for z in range(depth)]
            kv_passed = lax.ppermute(kv_passed, ("zh", "zl"), route)
        kv_pair = jnp.stack([kv, kv_passed])
        kv_all = lax.all_gather(kv_pair, "y", axis=0)
        arrived, kv_pair = lax.optimization_barrier((arrived, kv_pair))

    with jax.named_scope("experts"):
        answers = pl.pallas_call(
            functools.partial(expert_kernel, hidden_units),
            out_shape=jax.ShapeDtypeStruct((slots, wide), BF16),
            in_specs=[VMEM, HBM],
            out_specs=VMEM,
            scratch_shapes=[pltpu.VMEM(weights.shape, BF16), pltpu.SemaphoreType.DMA((4,))],
            compiler_params=params,
            cost_estimate=estimate(6 * 512 * 2048 * 384, 8 * 1024 * 1024),
            name="experts",
        )(arrived, weights)
        returned = lax.all_to_all(
            answers.reshape(owners, LOW, wide), CHIPS, split_axis=0, concat_axis=0, tiled=True
        ).reshape(slots, wide)

    with jax.named_scope("attend"):
        place = lax.axis_index(CTX).astype(jnp.int32)[None]
        attended = pl.pallas_call(
            functools.partial(attend_kernel, halves, ring, heads_kv),
            out_shape=jax.ShapeDtypeStruct(queries.shape[1:], BF16),
            in_specs=[VMEM, HBM, SMEM],
            out_specs=VMEM,
            scratch_shapes=[
                pltpu.VMEM((halves, ring, tokens, 2 * heads_kv * HD), BF16),
                pltpu.SemaphoreType.DMA((2,)),
            ],
            compiler_params=pltpu.CompilerParams(vmem_limit_bytes=60 * 1024 * 1024),
            cost_estimate=estimate(4 * 2048 * 128 * 2048, 4 * 1024 * 1024, 16 * 128 * 2048),
            name="attend",
        )(queries[0], kv_all, place)

    with jax.named_scope("combine"):
        expert_out = pl.pallas_call(
            functools.partial(combine_kernel, cores, ring),
            out_shape=jax.ShapeDtypeStruct((tokens, width), BF16),
            in_specs=[VMEM] * 3,
            out_specs=VMEM,
            compiler_params=params,
            cost_estimate=estimate(2 * 256 * 512 * 2048, 3 * 1024 * 1024),
            name="combine",
        )(returned, mix_a, mix_b)
    return (attended[None], expert_out[None])


def solution(mesh):
    fine = Mesh(mesh.devices.reshape(2, 8, 4, 4, 2), CTX + DP)
    rows = P(DP, CTX, None)
    return jax.shard_map(
        shards,
        mesh=fine,
        in_specs=(rows, rows, rows, rows, P(), rows, rows, rows, rows, P(DP, None, CTX)),
        out_specs=(rows, rows),
        check_vma=False,
    )
```

```python
import functools
import math

import jax
import jax.numpy as jnp
from jax import lax
from jax.experimental import pallas as pl
from jax.experimental.pallas import tpu as pltpu
from jax.sharding import Mesh, PartitionSpec as P

HD = 128
CAP = 12
LOW = 8
FOLD = CAP - LOW
CTX = ("zh", "y")
DP = ("zl", "x", "c")
CHIPS = ("zh", "zl", "x")
MASKED = -1e30
F32 = jnp.float32
BF16 = jnp.bfloat16
VMEM = pl.BlockSpec(memory_space=pltpu.VMEM)
HBM = pl.BlockSpec(memory_space=pltpu.HBM)
SMEM = pl.BlockSpec(memory_space=pltpu.SMEM)


def pack_kernel(gate_ref, up_ref, down_ref, out_ref, held_ref, in_sems, out_sems):
    rows, units = gate_ref.shape
    pieces = [(gate_ref, 0, units), (up_ref, units, units)]
    for j in range(units // rows):
        pieces.append((down_ref.at[pl.ds(j * rows, rows)], 2 * units + j * rows, rows))
    arriving, leaving = [], []
    for i, (source, start, columns) in enumerate(pieces):
        held = held_ref.at[:, pl.ds(start, columns)]
        arriving.append(pltpu.make_async_copy(source, held, in_sems.at[i]))
        leaving.append(pltpu.make_async_copy(held, out_ref.at[:, pl.ds(start, columns)], out_sems.at[i]))
        arriving[i].start()
    for i in range(len(pieces)):
        arriving[i].wait()
        leaving[i].start()
    for copy in leaving:
        copy.wait()


def host_place(z, core, depth, halves):
    return (z + depth // 2 + core * depth) % (depth * halves)


def natural_block(place, cores, ring):
    return (place % cores) * ring + place // cores


def dispatch_kernel(halves, depth, cores, ring, owners, x_ref, gain_ref, ids_ref, gates_ref, out_ref, mix_a_ref, mix_b_ref):
    tokens, width = x_ref.shape
    slots = owners * LOW
    half = width // 2
    x = x_ref[...].astype(F32)
    normed = (x * lax.rsqrt(jnp.mean(x * x, axis=-1, keepdims=True) + 1e-06) * gain_ref[...]).astype(BF16)
    step = width // (cores * ring)
    pieces = []
    for place in range(cores * ring):
        start = natural_block(place, cores, ring) * step
        pieces.append(normed[:, start : start + step])
    normed = jnp.concatenate(pieces, axis=1)

    lane = lax.broadcasted_iota(jnp.int32, (tokens, slots), 1)
    chip = lane // LOW
    across = owners // (halves * depth)
    turn = (chip // across + halves * depth - depth // 2) % (halves * depth)
    expert = (turn % depth * across + chip % across) * cores + turn // depth
    place = lane % LOW
    ids = ids_ref[...].T
    gates = gates_ref[...].T
    hot = jnp.zeros((tokens, slots), F32)
    gate = jnp.zeros((tokens, slots), F32)
    for k in range(ids.shape[1]):
        hit = ids[:, k : k + 1] == expert
        hot = jnp.where(hit, 1.0, hot)
        gate = jnp.where(hit, gates[:, k : k + 1], gate)
    row = lax.broadcasted_iota(jnp.int32, (tokens, tokens), 0)
    col = lax.broadcasted_iota(jnp.int32, (tokens, tokens), 1)
    earlier = jnp.where(col < row, 1.0, 0.0).astype(BF16)
    rank = jnp.dot(earlier, hot.astype(BF16), preferred_element_type=F32)
    rank = jnp.where(hot > 0.5, rank, -1.0)
    in_a = rank == place.astype(F32)
    in_b = rank == (LOW + place % FOLD).astype(F32)
    in_lo = in_b & (place < FOLD)
    in_hi = in_b & (place >= FOLD)

    def put(chosen):
        return jnp.where(chosen, 1.0, 0.0).astype(BF16)

    contract = (((0,), (0,)), ((), ()))
    out_ref[:, :width] = lax.dot_general(put(in_a), normed, contract, preferred_element_type=F32).astype(BF16)
    pick = jnp.concatenate([put(in_lo), put(in_hi)], axis=0)
    stacked = jnp.concatenate([normed[:, :half], normed[:, half:]], axis=0)
    out_ref[:, width:] = lax.dot_general(pick, stacked, contract, preferred_element_type=F32).astype(BF16)

    top = gate.astype(BF16).astype(F32)
    rest = gate - top

    def mix(chosen):
        return jnp.concatenate(
            [jnp.where(chosen, top, 0.0).astype(BF16), jnp.where(chosen, rest, 0.0).astype(BF16)], axis=0
        )

    mix_a_ref[...] = mix(in_a)
    mix_b_ref[:, :slots] = mix(in_lo)
    mix_b_ref[:, slots:] = mix(in_hi)


def expert_kernel(hidden_units, x_ref, w_hbm, out_ref, w_ref, sems):
    rows, cols = x_ref.shape
    width = w_ref.shape[0] * w_ref.shape[1]
    half = width // 2
    both = 2 * hidden_units
    block = w_ref.shape[1]
    count = w_ref.shape[0]

    chunks = sems.shape[0]
    per = count // chunks
    copies = []
    for i in range(chunks):
        at = pl.ds(i * per, per)
        copies.append(pltpu.make_async_copy(w_hbm.at[at], w_ref.at[at], sems.at[i]))
        copies[-1].start()
    sums_a, folds = None, [None, None]
    for i in range(chunks):
        copies[i].wait()
        piece = w_ref[i * per : (i + 1) * per, :, :both].reshape(per * block, both)
        start, side = i * per * block, 2 * i // chunks
        more = jnp.dot(x_ref[:, start : start + per * block], piece, preferred_element_type=F32)
        sums_a = more if sums_a is None else sums_a + more
        start = width + start - side * half
        more = jnp.dot(x_ref[:, start : start + per * block], piece, preferred_element_type=F32)
        folds[side] = more if folds[side] is None else folds[side] + more
    first = lax.broadcasted_iota(jnp.int32, (rows, both), 0) % LOW < FOLD
    sums_b = jnp.where(first, folds[0], folds[1])
    groups = sums_b.reshape(rows // LOW, LOW, both)
    sums_b = (groups + pltpu.roll(groups, FOLD, 1)).reshape(rows, both)

    def activate(sums):
        gate = sums[:, :hidden_units]
        return (gate / (1.0 + jnp.exp(-gate)) * sums[:, hidden_units:]).astype(BF16)

    hidden_a = activate(sums_a)
    hidden_b = activate(sums_b)

    def down(place):
        pieces = [w_ref[place, :, both + j * block : both + (j + 1) * block] for j in range(hidden_units // block)]
        return jnp.concatenate(pieces, axis=0)

    first_out = lax.broadcasted_iota(jnp.int32, (rows, 2 * block), 0) % LOW < FOLD
    for pair in range(count // 4):
        lo, hi = 2 * pair, count // 2 + 2 * pair
        low_d = jnp.concatenate([down(lo), down(lo + 1)], axis=1)
        high_d = jnp.concatenate([down(hi), down(hi + 1)], axis=1)
        out_ref[:, lo * block : (lo + 2) * block] = jnp.dot(
            hidden_a, low_d, preferred_element_type=F32
        ).astype(BF16)
        out_ref[:, hi * block : (hi + 2) * block] = jnp.dot(
            hidden_a, high_d, preferred_element_type=F32
        ).astype(BF16)
        out_ref[:, width + lo * block : width + (lo + 2) * block] = jnp.where(
            first_out,
            jnp.dot(hidden_b, low_d, preferred_element_type=F32),
            jnp.dot(hidden_b, high_d, preferred_element_type=F32),
        ).astype(BF16)


def combine_kernel(cores, ring, back_ref, mix_a_ref, mix_b_ref, out_ref):
    tokens, width = out_ref.shape
    half = width // 2
    slots = back_ref.shape[0]
    step = width // (cores * ring)
    folded = back_ref[:, width:]
    for side in range(2):
        both = jnp.dot(
            mix_a_ref[...], back_ref[:, side * half : (side + 1) * half], preferred_element_type=F32
        ) + jnp.dot(
            mix_b_ref[:, side * slots : (side + 1) * slots], folded, preferred_element_type=F32
        )
        total = (both[:tokens] + both[tokens:]).astype(BF16)
        for i in range(half // step):
            start = natural_block(side * (half // step) + i, cores, ring) * step
            out_ref[:, start : start + step] = total[:, i * step : (i + 1) * step]


def attend_kernel(halves, ring, heads_kv, q_ref, kv_hbm, place_ref, out_ref, kv_ref, sems):
    tokens, wide = q_ref.shape
    group = wide // HD // heads_kv
    keys = ring * tokens
    kind = heads_kv * HD
    factor = math.log2(math.e) / math.sqrt(HD)
    copies = []
    for side in range(halves):
        copies.append(pltpu.make_async_copy(kv_hbm.at[:, side], kv_ref.at[side], sems.at[side]))
        copies[side].start()
    here = place_ref[0] // ring
    mine = place_ref[0] % ring
    lane = lax.broadcasted_iota(jnp.int32, (tokens, keys), 1)
    row = lax.broadcasted_iota(jnp.int32, (tokens, keys), 0)
    bias = jnp.where(lane <= row + mine * tokens, 0.0, MASKED)
    for copy in copies:
        copy.wait()

    def attend(sides):
        ones = jnp.ones((sides * keys, HD), BF16)
        for g in range(heads_kv):
            key = kv_ref[:sides, :, :, g * HD : (g + 1) * HD].reshape(sides * keys, HD)
            value = kv_ref[:sides, :, :, kind + g * HD : kind + (g + 1) * HD].reshape(sides * keys, HD)
            value = jnp.concatenate([value, ones], axis=1)
            for i in range(g * group, (g + 1) * group):
                at = slice(i * HD, (i + 1) * HD)
                scores = lax.dot_general(
                    q_ref[:, at], key, (((1,), (1,)), ((), ())), preferred_element_type=F32
                )
                scores = scores * factor
                masked = scores[:, :keys] + bias
                scores = masked if sides == 1 else jnp.concatenate([masked, scores[:, keys:]], axis=1)
                probs = jnp.exp2(scores - jnp.max(scores, axis=-1, keepdims=True))
                mixed = jnp.dot(probs.astype(BF16), value, preferred_element_type=F32)
                out_ref[:, at] = (mixed[:, :HD] / mixed[:, HD:]).astype(BF16)

    @pl.when(here == 0)
    def _():
        attend(1)

    @pl.when(here > 0)
    def _():
        attend(halves)


def estimate(flops, bytes_accessed, transcendentals=0):
    return pl.CostEstimate(flops=flops, bytes_accessed=bytes_accessed, transcendentals=transcendentals)


def shards(
    queries, key_rows, value_rows, stream, norm_gain, expert_ids, gate_values, w_gate, w_up, w_down
):
    tokens, width = stream.shape[1:]
    heads_kv = key_rows.shape[2] // HD
    hidden_units = w_gate.shape[2]
    halves, ring, cores = lax.axis_size("zh"), lax.axis_size("y"), lax.axis_size("c")
    depth = lax.axis_size("zl")
    owners = lax.axis_size(DP)
    slots = owners * LOW
    wide = width + width // 2
    params = pltpu.CompilerParams(vmem_limit_bytes=48 * 1024 * 1024)

    with jax.named_scope("weights"):
        packed = pl.pallas_call(
            pack_kernel,
            out_shape=jax.ShapeDtypeStruct((w_gate.shape[1], 3 * hidden_units), BF16),
            in_specs=[HBM] * 3,
            out_specs=HBM,
            scratch_shapes=[
                pltpu.VMEM((w_gate.shape[1], 3 * hidden_units), BF16),
                pltpu.SemaphoreType.DMA((2 + hidden_units // tokens,)),
                pltpu.SemaphoreType.DMA((2 + hidden_units // tokens,)),
            ],
            name="pack",
        )(w_gate[0], w_up[0], w_down[0])
        route = []
        for h in range(halves):
            for z in range(depth):
                for c in range(cores):
                    to = host_place(z, c, depth, halves)
                    route.append(((h * depth + z) * cores + c, to * cores + h))
        part = lax.ppermute(packed, ("zh", "zl", "c"), route)
    with jax.named_scope("dispatch"):
        ids, _ = lax.optimization_barrier((expert_ids[0].T, packed))
        outgoing, mix_a, mix_b = pl.pallas_call(
            functools.partial(dispatch_kernel, halves, depth, cores, ring, owners),
            out_shape=(
                jax.ShapeDtypeStruct((slots, wide), BF16),
                jax.ShapeDtypeStruct((2 * tokens, slots), BF16),
                jax.ShapeDtypeStruct((2 * tokens, 2 * slots), BF16),
            ),
            in_specs=[VMEM] * 4,
            out_specs=(VMEM,) * 3,
            compiler_params=pltpu.CompilerParams(vmem_limit_bytes=65200 * 1024),
            cost_estimate=estimate(4 * 256 * 256 * 2048, 4 * 1024 * 1024),
            name="dispatch",
        )(stream[0], norm_gain[None, :], ids, gate_values[0].T)
        arrived = lax.all_to_all(
            outgoing.reshape(owners, LOW, wide), CHIPS, split_axis=0, concat_axis=0, tiled=True
        ).reshape(slots, wide)

    with jax.named_scope("keys"):
        key_local, value_local, _ = lax.optimization_barrier((key_rows[0], value_rows[0], outgoing))
        kv = jnp.concatenate([key_local, value_local], axis=1)
        part, kv = lax.optimization_barrier((part, kv))
        weights = lax.all_gather(part, ("y", "c"), axis=0)
        kv_passed = lax.ppermute(kv, "zh", [(0, 1)])
        kv_pair = jnp.stack([kv, kv_passed])
        kv_all = lax.all_gather(kv_pair, "y", axis=0)
        arrived, kv_pair = lax.optimization_barrier((arrived, kv_pair))

    with jax.named_scope("experts"):
        answers = pl.pallas_call(
            functools.partial(expert_kernel, hidden_units),
            out_shape=jax.ShapeDtypeStruct((slots, wide), BF16),
            in_specs=[VMEM, HBM],
            out_specs=VMEM,
            scratch_shapes=[pltpu.VMEM(weights.shape, BF16), pltpu.SemaphoreType.DMA((4,))],
            compiler_params=params,
            cost_estimate=estimate(6 * 512 * 2048 * 384, 8 * 1024 * 1024),
            name="experts",
        )(arrived, weights)
        returned = lax.all_to_all(
            answers.reshape(owners, LOW, wide), CHIPS, split_axis=0, concat_axis=0, tiled=True
        ).reshape(slots, wide)

    with jax.named_scope("attend"):
        place = lax.axis_index(CTX).astype(jnp.int32)[None]
        attended = pl.pallas_call(
            functools.partial(attend_kernel, halves, ring, heads_kv),
            out_shape=jax.ShapeDtypeStruct(queries.shape[1:], BF16),
            in_specs=[VMEM, HBM, SMEM],
            out_specs=VMEM,
            scratch_shapes=[
                pltpu.VMEM((halves, ring, tokens, 2 * heads_kv * HD), BF16),
                pltpu.SemaphoreType.DMA((2,)),
            ],
            compiler_params=pltpu.CompilerParams(vmem_limit_bytes=60 * 1024 * 1024),
            cost_estimate=estimate(4 * 2048 * 128 * 2048, 4 * 1024 * 1024, 16 * 128 * 2048),
            name="attend",
        )(queries[0], kv_all, place)

    with jax.named_scope("combine"):
        expert_out = pl.pallas_call(
            functools.partial(combine_kernel, cores, ring),
            out_shape=jax.ShapeDtypeStruct((tokens, width), BF16),
            in_specs=[VMEM] * 3,
            out_specs=VMEM,
            compiler_params=params,
            cost_estimate=estimate(2 * 256 * 512 * 2048, 3 * 1024 * 1024),
            name="combine",
        )(returned, mix_a, mix_b)
    return (attended[None], expert_out[None])


def solution(mesh):
    fine = Mesh(mesh.devices.reshape(2, 8, 4, 4, 2), CTX + DP)
    rows = P(DP, CTX, None)
    return jax.shard_map(
        shards,
        mesh=fine,
        in_specs=(rows, rows, rows, rows, P(), rows, rows, rows, rows, P(DP, None, CTX)),
        out_specs=(rows, rows),
        check_vma=False,
    )
```
